128 devices in a mesh: rows: 16 (over x, z_lo, core), cols: 8 (over z_hi, y).
Axes of the slice: x: 4, y: 4, z: 4 (z_hi: 2, z_lo: 2; z = z_hi * 2 + z_lo), core: 2. Of those that a mesh axis runs over, the one named last changes fastest.
Arguments:
- krylov: bfloat16 [32768, 256], P(('rows', 'cols')), may hold values from -6 to 6
- geometry: float32 [7, 32768], P(None, ('rows', 'cols')), may hold values from -1 to 2, as said below
- corr_index: int32 [8, 32768], P(None, ('rows', 'cols')), may hold values from 0 to 32767, as said below
- corr_weight: float32 [16, 32768], P(None, ('rows', 'cols')), may hold values from -1.5 to 1.5
- blades: int32 [128], replicated, may hold values from 3 to 8
- harmonic: int32 [128], replicated, may hold values from 1 to 4
- observer_angles: float32 [2, 8192], replicated, may hold values from -3.140625 to 3.140625
Outputs:
- residual: float32 [32768, 256], P(('rows', 'cols'))
- far_field: float32 [8192, 256], P(('rows', 'cols'))
The draws below stay inside these ranges and needn't reach their ends.
Inputs may be any that keep to these rules, and one draw needn't show every extreme that they name: `geometry`: centers lie on a duct of radius about 1 with heights 0 to 2 and on a centerbody of radius 0.35; normals have unit length; areas are positive. corr_index[c, i] lies in the same aligned block of 256 consecutive panels as panel i.
All inputs are finite; a program needn't handle non-finite values.
Results may differ from the reference program's by a relative error of at most 0.0029.
Values may be sent and summed in bfloat16 or wider, within the bound.
A program may use at most 64 MiB of HBM per device.

```python
import math
import jax
import jax.numpy as jnp
from jax import lax

PANELS_DEV = 256
NV = 128
NC = 8
NS = 64
NP = 32768
NOBS = 8192


def draw_geometry(key, part):
    keys = jax.random.split(jax.random.fold_in(key, 11), 5)
    choose = jax.random.uniform(keys[0], (NP,), jnp.float32)
    theta = jax.random.uniform(keys[1], (NP,), jnp.float32, 0.0, 2.0 * math.pi)
    height = jax.random.uniform(keys[2], (NP,), jnp.float32)
    slope = jax.random.uniform(keys[3], (NP,), jnp.float32, -0.2, 0.2)
    duct = choose < 0.7
    radius = jnp.where(duct, 1.0, 0.35)
    pos_z = jnp.where(duct, 2.0 * height, 0.3 + 1.4 * height)
    sign = jnp.where(duct, -1.0, 1.0)
    scale = 1.0 / jnp.sqrt(1.0 + slope * slope)
    spread = jax.random.uniform(keys[4], (NP,), jnp.float32, math.log(0.5), math.log(2.0))
    area = 16.0 / NP * jnp.exp(spread)
    return jnp.stack([radius * jnp.cos(theta), radius * jnp.sin(theta), pos_z, sign * jnp.cos(theta) * scale, sign * jnp.sin(theta) * scale, slope * scale, area]).astype(jnp.float32)


def draw_corr_index(key, part):
    offsets = jax.random.randint(jax.random.fold_in(key, 23), (NC, NP), 0, PANELS_DEV, dtype=jnp.int32)
    base = jnp.arange(NP, dtype=jnp.int32) // PANELS_DEV * PANELS_DEV
    return (base[None, :] + offsets).astype(jnp.int32)


def set_ends(values, key, least, largest):
    shape = values.shape
    place = [jax.random.randint(jax.random.fold_in(key, axis), (), 0, shape[axis]) for axis in range(len(shape))]
    values = values.at[tuple(place)].set(least)
    longest = shape.index(max(shape))
    place[longest] = (place[longest] + 1) % shape[longest]
    return values.at[tuple(place)].set(largest)


def level_of(stream_key, dims, cuts, least, high):
    def one(axis_at, shards_of):
        draws = jax.random.uniform(jax.random.fold_in(jax.random.fold_in(stream_key, 6), axis_at), (shards_of,), jnp.float32, least / len(cuts), high / len(cuts))
        return jnp.repeat(jnp.exp(draws), dims[axis_at] // shards_of).reshape((-1,) + (1,) * (len(dims) - axis_at - 1))

    factor_of = one(*cuts[0])
    for cut in cuts[1:]:
        factor_of = factor_of * one(*cut)
    return factor_of


def noise(rng, shape, scale, reach, pieces=(), held_as=jnp.bfloat16):
    array = scale * jax.random.normal(rng, shape, jnp.float32)
    if pieces:
        array = array * level_of(rng, shape, pieces, -0.22, 0.18)
    return jnp.clip(array, -reach, reach).astype(held_as)


def setup_inputs(seed: int = 0) -> dict:
    seeds = jax.random.split(jax.random.key(seed), 8)
    krylov = noise(seeds[0], (NP, 2 * NV), 1.0, 6.0, ((0, 128),))
    geometry = draw_geometry(jax.random.fold_in(seeds[7], 71), 0)
    corr_index = draw_corr_index(jax.random.fold_in(seeds[7], 71), 0)
    corr_weight = noise(seeds[3], (2 * NC, NP), 0.3, 1.5, ((1, 128),), jnp.float32)
    blades = set_ends(jax.random.randint(seeds[4], (NV,), 3, 9), jax.random.fold_in(seeds[4], 1), 3, 8).astype(jnp.int32)
    harmonic = set_ends(jax.random.randint(seeds[5], (NV,), 1, 5), jax.random.fold_in(seeds[5], 1), 1, 4).astype(jnp.int32)
    observer_angles = jnp.clip(jax.random.uniform(seeds[6], (2, NOBS), jnp.float32, -3.140625, 3.140625), -3.140625, 3.140625)
    return {"krylov": krylov, "geometry": geometry, "corr_index": corr_index, "corr_weight": corr_weight, "blades": blades, "harmonic": harmonic, "observer_angles": observer_angles}


wavenumber = 20.0
cycle_radius = 0.7
cycle_height = 1.0
four_pi = 4.0 * math.pi

def green_parts(r_sq):
    inverse = lax.rsqrt(r_sq)
    phase = wavenumber * r_sq * inverse
    g_re = jnp.cos(phase) * inverse / four_pi
    g_im = jnp.sin(phase) * inverse / four_pi
    f_re = (-g_re * inverse - wavenumber * g_im) * inverse
    f_im = (-g_im * inverse + wavenumber * g_re) * inverse
    return (g_re, g_im, f_re, f_im)

def panel_tile(row_geom, col_geom, row_ids, col_ids, soft_sq):
    dx = row_geom[0][:, None] - col_geom[0][None, :]
    dy = row_geom[1][:, None] - col_geom[1][None, :]
    dz = row_geom[2][:, None] - col_geom[2][None, :]
    r_sq = dx * dx + dy * dy + dz * dz + soft_sq
    g_re, g_im, f_re, f_im = green_parts(r_sq)
    along_col = -(dx * col_geom[3][None, :] + dy * col_geom[4][None, :] + dz * col_geom[5][None, :])
    along_row = (dx * row_geom[3][:, None] + dy * row_geom[4][:, None] + dz * row_geom[5][:, None]) / wavenumber
    area = col_geom[6][None, :]
    t_re = area * (f_re * along_col - f_im * along_row)
    t_im = area * (f_re * along_row + f_im * along_col)
    same = row_ids[:, None] == col_ids[None, :]
    zeros = jnp.zeros_like(t_re)
    return (jnp.where(same, zeros, t_re).astype(jnp.bfloat16), jnp.where(same, zeros, t_im).astype(jnp.bfloat16))

def apply_tile(t_re, t_im, vectors):
    nvec = vectors.shape[1] // 2
    first = jnp.dot(t_re, vectors, preferred_element_type=jnp.float32)
    second = jnp.dot(t_im, vectors, preferred_element_type=jnp.float32)
    return jnp.concatenate([first[:, :nvec] - second[:, nvec:], first[:, nvec:] + second[:, :nvec]], axis=1)

def far_tile(angles, geom):
    sin_t = jnp.sin(angles[0])
    dir_x = sin_t * jnp.cos(angles[1])
    dir_y = sin_t * jnp.sin(angles[1])
    dir_z = jnp.cos(angles[0])
    along = dir_x[:, None] * geom[0][None, :] + dir_y[:, None] * geom[1][None, :] + dir_z[:, None] * geom[2][None, :]
    normal_part = dir_x[:, None] * geom[3][None, :] + dir_y[:, None] * geom[4][None, :] + dir_z[:, None] * geom[5][None, :]
    phase = -wavenumber * along
    scale = geom[6][None, :] * wavenumber * normal_part
    t_re = scale * jnp.sin(phase)
    t_im = -scale * jnp.cos(phase)
    return (t_re.astype(jnp.bfloat16), t_im.astype(jnp.bfloat16))

def incident(geom, blades, harmonic):
    angle = 2.0 * math.pi * jnp.arange(NS, dtype=jnp.float32) / NS
    src_x = cycle_radius * jnp.cos(angle)
    src_y = cycle_radius * jnp.sin(angle)
    dx = geom[0][:, None] - src_x[None, :]
    dy = geom[1][:, None] - src_y[None, :]
    dz = geom[2][:, None] - cycle_height
    r_sq = dx * dx + dy * dy + dz * dz
    g_re, g_im, f_re, f_im = green_parts(r_sq)
    normal_part = (dx * geom[3][:, None] + dy * geom[4][:, None] + dz * geom[5][:, None]) / wavenumber
    h_re = g_re - f_im * normal_part
    h_im = g_im + f_re * normal_part
    modes = (blades * harmonic).astype(jnp.float32)
    e_re = jnp.cos(angle[:, None] * modes[None, :])
    e_im = jnp.sin(angle[:, None] * modes[None, :])
    high = lax.Precision.HIGHEST
    b_re = jnp.dot(h_re, e_re, precision=high) - jnp.dot(h_im, e_im, precision=high)
    b_im = jnp.dot(h_re, e_im, precision=high) + jnp.dot(h_im, e_re, precision=high)
    return jnp.concatenate([b_re, b_im], axis=1)

def correction(values, index_local, weights):
    count = index_local.shape[0]
    nvec = values.shape[1] // 2
    nearby = values[index_local]
    w_re = weights[:count][:, :, None]
    w_im = weights[count:][:, :, None]
    part_re = lax.optimization_barrier(jnp.sum(w_re * nearby[:, :, :nvec] - w_im * nearby[:, :, nvec:], axis=0))
    part_im = lax.optimization_barrier(jnp.sum(w_re * nearby[:, :, nvec:] + w_im * nearby[:, :, :nvec], axis=0))
    return jnp.concatenate([part_re, part_im], axis=1)

def reference(krylov, geometry, corr_index, corr_weight, blades, harmonic, observer_angles):
    soft_sq = 4.0 / NP
    panel_ids = jnp.arange(NP, dtype=jnp.int32)
    row_block = math.gcd(NP, 512)

    def one_block(step):
        start = (step * row_block).astype(jnp.int32)
        geom = lax.dynamic_slice_in_dim(geometry, start, row_block, 1)
        ids = lax.dynamic_slice_in_dim(panel_ids, start, row_block, 0)
        t_re, t_im = panel_tile(geom, geometry, ids, panel_ids, soft_sq)
        return apply_tile(t_re, t_im, krylov)
    applied = lax.map(one_block, jnp.arange(NP // row_block, dtype=jnp.int32)).reshape(NP, 2 * NV)
    values = krylov.astype(jnp.float32)
    near = correction(values, corr_index, corr_weight)
    source = incident(geometry, blades, harmonic)
    residual = source - (0.5 * values + near + applied)
    obs_block = math.gcd(NOBS, 512)

    def one_far(step):
        start = (step * obs_block).astype(jnp.int32)
        angles = lax.dynamic_slice_in_dim(observer_angles, start, obs_block, 1)
        t_re, t_im = far_tile(angles, geometry)
        return apply_tile(t_re, t_im, krylov)
    far_field = lax.map(one_far, jnp.arange(NOBS // obs_block, dtype=jnp.int32)).reshape(NOBS, 2 * NV)
    return (residual, far_field)
```

```python
import functools
import math

import jax
import jax.numpy as jnp
from jax import lax
from jax.experimental import pallas as pl
from jax.experimental.pallas import tpu as pltpu
from jax.sharding import PartitionSpec as P

BF = jnp.bfloat16
F32 = jnp.float32
NS = 64
LANES = 128

wavenumber = 20.0
cycle_radius = 0.7
cycle_height = 1.0
four_pi = 4.0 * math.pi
two_pi = 2.0 * math.pi
kappa = wavenumber / two_pi

dot = functools.partial(jnp.dot, preferred_element_type=F32)


def pieces(x):
    first = x.astype(BF).astype(F32)
    rest = x - first
    second = rest.astype(BF).astype(F32)
    return first, second, (rest - second).astype(BF).astype(F32)


def left_stack(x):
    a, b, c = pieces(x)
    return jnp.concatenate([a, a, b, a, c, b], axis=0)


def right_stack(x):
    a, b, c = pieces(x)
    return jnp.concatenate([a, b, a, c, a, b], axis=0).astype(BF)


def panel_rows(g):
    row = lax.broadcasted_iota(jnp.int32, g.shape, 0)
    center = row < 3
    normal = pltpu.roll(g, 5, 0)
    c_sq = jnp.sum(jnp.where(center, g * g, 0.0), axis=0, keepdims=True)
    n_c = jnp.sum(jnp.where(center, g * normal, 0.0), axis=0, keepdims=True)
    return row, center, normal, c_sq, n_c, g[6:7]


def left_features(g, soft_sq):
    row, center, normal, c_sq, n_c, _ = panel_rows(g)
    size = (kappa * kappa) * (c_sq + soft_sq)
    one = jnp.where(row == 3, 1.0, jnp.where(row == 4, size, 0.0))
    two = jnp.where(row == 3, n_c, 0.0)
    return (
        left_stack(jnp.where(center, g, one)),
        left_stack(jnp.where(center, normal, two)),
    )


def right_features(g):
    row, center, normal, c_sq, n_c, area = panel_rows(g)
    scale = area * (kappa * kappa / four_pi)
    k_sq = kappa * kappa
    r_sq = jnp.where(
        center, -2.0 * k_sq * g, jnp.where(row == 3, k_sq * c_sq, jnp.where(row == 4, 1.0, 0.0))
    )
    along_col = jnp.where(
        center, -wavenumber * scale * normal, jnp.where(row == 3, wavenumber * scale * n_c, 0.0)
    )
    along_row = jnp.where(center, scale * g, jnp.where(row == 3, -scale, 0.0))
    far_turns = jnp.where(center, kappa * g, 0.0)
    far_scale = jnp.where(center, -wavenumber * area * normal, 0.0)
    return [right_stack(v) for v in (r_sq, along_col, along_row, far_turns, far_scale)]


def operator_tile(r_sq, along_col, along_row):
    inv = lax.rsqrt(r_sq)
    turns = r_sq * inv
    part = (turns - jnp.round(turns)).astype(BF)
    u = inv.astype(BF)
    a = along_col.astype(BF)
    b = along_row.astype(BF)

    def const(v):
        return jnp.asarray(v, BF)

    z = part * part
    sin_poly = (z * const(SIN[2]) + const(SIN[1])) * z + const(SIN[0])
    cos_poly = (z * const(COS[2]) + const(COS[1])) * z + const(COS[0])
    s = (part * u) * sin_poly
    c = u * cos_poly
    re = u * u - s * s
    im = s * c
    w = u * const(1.0 / two_pi)
    p = b - w * a
    q = a + w * b
    return re * p - im * q, re * q + im * p


root2 = math.sqrt(2.0)
SIN = [root2 * v for v in (3.14064003, -5.1369052, 2.29954689)]
COS = [root2 * v for v in (0.99940322, -4.89118661, 3.5838431)]


def far_values(turns, scale):
    part = turns - jnp.round(turns)
    z = part * part
    s = part * (((z * -0.55463616 + 2.54189901) * z + -5.16714279) * z + 3.14158202)
    c = ((z * -1.22212692 + 4.04128377) * z + -4.93393801) * z + 0.9999933
    s2 = s + s
    return (scale * (s2 * c)).astype(BF), (scale * (1.0 - s2 * s)).astype(BF)


def sin_cos(turns):
    part = turns - jnp.round(turns)
    quarter = jnp.round(4.0 * part)
    y = (part - 0.25 * quarter) * two_pi
    z = y * y
    s = y * (1.0 + z * (-1.0 / 6 + z * (1.0 / 120 + z * (-1.0 / 5040 + z * (1.0 / 362880)))))
    c = 1.0 + z * (-0.5 + z * (1.0 / 24 + z * (-1.0 / 720 + z * (1.0 / 40320))))
    odd = jnp.abs(quarter) == 1.0
    sin_v = jnp.where(odd, c, s)
    cos_v = jnp.where(odd, s, c)
    sin_v = jnp.where((quarter == -1.0) | (jnp.abs(quarter) == 2.0), -sin_v, sin_v)
    cos_v = jnp.where((quarter == 1.0) | (jnp.abs(quarter) == 2.0), -cos_v, cos_v)
    return sin_v, cos_v


ROWS = 512
COLS = 512
SUB = 16


def compute(row_geom, col_geom, vectors, angles, own, out, far_out, left_a, left_b, rights, x2, planes, tiles, acc):
    n_rows = row_geom.shape[1]
    n_cols = col_geom.shape[1]
    steps = n_cols // COLS
    half = COLS // LANES
    soft_sq = 4.0 / own[2]

    la, lb = left_features(row_geom[...], soft_sq)
    left_a[pl.ds(0, n_rows), :] = la.T.astype(BF)
    left_b[...] = lb.T.astype(BF)
    t, p = angles[0:1, :] * (1.0 / two_pi), angles[1:2, :] * (1.0 / two_pi)
    sin_t, cos_t = sin_cos(t)
    sin_p, cos_p = sin_cos(p)
    e = jnp.concatenate([sin_t * cos_p, sin_t * sin_p, cos_t, jnp.zeros((5, t.shape[1]), F32)], axis=0)
    left_a[pl.ds(n_rows, t.shape[1]), :] = left_stack(e).T.astype(BF)
    for ref, v in zip(rights, right_features(col_geom[...])):
        ref[...] = v
    for i in range(steps):
        x = vectors[pl.ds(i * COLS, COLS), :]
        x2[pl.ds(i * 2 * COLS, COLS), :] = x
        x2[pl.ds(i * 2 * COLS + COLS, COLS), :] = jnp.concatenate([-x[:, LANES:], x[:, :LANES]], axis=1)

    def geometry(first, step, far, into):
        cols = pl.ds(pl.multiple_of(step * COLS, COLS), COLS)
        la = left_a[pl.ds(pl.multiple_of(first, ROWS), ROWS), :]
        if far:
            into[0][...] = dot(la, rights[3][:, cols])
            into[1][...] = dot(la, rights[4][:, cols])
        else:
            lb = left_b[pl.ds(pl.multiple_of(first, ROWS), ROWS), :]
            into[0][...] = dot(la, rights[0][:, cols])
            into[1][...] = dot(la, rights[1][:, cols])
            into[2][...] = dot(lb, rights[2][:, cols])

    def values(step, far, frm, tile):
        for r in range(0, ROWS, SUB):
            rows = pl.ds(r, SUB)
            if far:
                re, im = far_values(frm[0][rows, :], frm[1][rows, :])
            else:
                re, im = operator_tile(frm[0][rows, :], frm[1][rows, :], frm[2][rows, :])
            for h in range(half):
                tile[step * 2 * half + h, rows, :] = re[:, h * LANES:(h + 1) * LANES]
                tile[step * 2 * half + half + h, rows, :] = im[:, h * LANES:(h + 1) * LANES]

    def product(step, tile):
        lhs = jnp.concatenate([tile[step * 2 * half + h] for h in range(2 * half)], axis=1)
        xs = pl.ds(pl.multiple_of(step * 2 * COLS, 2 * COLS), 2 * COLS)
        acc[...] += dot(lhs, x2[xs, :])

    blocks = n_rows // ROWS
    seq = [(n_rows, True)] + [(b * ROWS, False) for b in range(blocks)]
    for ph in range(len(seq) + 1):
        gen = ph < len(seq)
        mul = ph > 0
        if gen:
            first, far = seq[ph]
            geometry(first, 0, far, planes[0])
        if mul:
            acc[...] = jnp.zeros_like(acc)

        @pl.loop(0, steps // 2)
        def _(h):
            for par in range(2):
                step = 2 * h + par
                if gen:
                    geometry(first, lax.rem(step + 1, steps), far, planes[1 - par])
                    values(step, far, planes[par], tiles[ph % 2])
                if mul:
                    product(step, tiles[(ph - 1) % 2])

        if gen and not far:
            @pl.when(own[0] // ROWS == first // ROWS)
            def _():
                rows = pl.ds(pl.multiple_of(own[0] % ROWS, 256), 256)
                same = lax.broadcasted_iota(jnp.int32, (256, LANES), 0)
                lane = lax.broadcasted_iota(jnp.int32, (256, LANES), 1)
                for h in range(2):
                    for part in range(2):
                        at = own[1] // COLS * 2 * half + part * half + own[1] % COLS // LANES + h
                        v = tiles[ph % 2][at, rows, :].astype(F32)
                        tiles[ph % 2][at, rows, :] = jnp.where(same == lane + h * LANES, 0.0, v).astype(BF)
        if mul:
            first, far = seq[ph - 1]
            if far:
                far_out[...] = acc[...]
            else:
                out[pl.ds(first, ROWS), :] = acc[...]


def tile_products(row_geom, col_geom, vectors, angles, row_first, col_first, panels):
    n_rows, n_cols, n_obs = row_geom.shape[1], col_geom.shape[1], angles.shape[1]
    pad = lambda g: jnp.concatenate([g, jnp.zeros((1, g.shape[1]), F32)], axis=0)

    def body(own_ref, rg, cg, x, an, out, far_out, la, lb, r0, r1, r2, r3, r4, x2, p0, p1, p2, p3, p4, p5, t0, t1, acc):
        compute(rg, cg, x, an, (own_ref[0], own_ref[1], panels), out, far_out, la, lb, (r0, r1, r2, r3, r4), x2,
                ((p0, p1, p2), (p3, p4, p5)), (t0, t1), acc)

    vm = pl.BlockSpec(memory_space=pltpu.VMEM)
    return pl.pallas_call(
        body,
        out_shape=(jax.ShapeDtypeStruct((n_rows, 256), F32), jax.ShapeDtypeStruct((n_obs, 256), F32)),
        in_specs=[pl.BlockSpec(memory_space=pltpu.SMEM), vm, vm, vm, vm],
        out_specs=(vm, vm),
        scratch_shapes=[pltpu.VMEM((n_rows + n_obs, 48), BF), pltpu.VMEM((n_rows, 48), BF)]
        + [pltpu.VMEM((48, n_cols), BF)] * 5
        + [pltpu.VMEM((2 * n_cols, 256), BF)]
        + [pltpu.VMEM((ROWS, COLS), F32)] * 6
        + [pltpu.VMEM((2 * n_cols // LANES, ROWS, LANES), BF)] * 2
        + [pltpu.VMEM((ROWS, 256), F32)],
        compiler_params=pltpu.CompilerParams(vmem_limit_bytes=60 << 20),
        name="tile_products",
    )(jnp.stack([row_first, col_first]).astype(jnp.int32), pad(row_geom), pad(col_geom), vectors, angles)


def in_order(tiles, dim):
    tiles = jnp.moveaxis(tiles, 0, dim)
    shape = tiles.shape
    return tiles.reshape(*shape[:dim], shape[dim] * shape[dim + 1], *shape[dim + 2 :])


def from_everyone(x, axis):
    devices = lax.axis_size(axis)
    return lax.all_to_all(jnp.broadcast_to(x[None], (devices, *x.shape)), axis, 0, 0, tiled=True)


def collect(x, axis, dim):
    return in_order(from_everyone(x, axis), dim)


def cut_along(x, dim, devices):
    shape = x.shape
    tiles = x.reshape(*shape[:dim], devices, shape[dim] // devices, *shape[dim + 1 :])
    return jnp.moveaxis(tiles, dim, 0)


def sent_and_summed(x, axis, dim):
    devices = lax.axis_size(axis)
    tiles = lax.all_to_all(cut_along(x, dim, devices), axis, 0, 0, tiled=True)
    return jnp.sum(tiles, axis=0)


def green_parts(r_sq):
    inverse = lax.rsqrt(r_sq)
    phase = wavenumber * r_sq * inverse
    g_re = jnp.cos(phase) * inverse / four_pi
    g_im = jnp.sin(phase) * inverse / four_pi
    f_re = (-g_re * inverse - wavenumber * g_im) * inverse
    f_im = (-g_im * inverse + wavenumber * g_re) * inverse
    return (g_re, g_im, f_re, f_im)


def incident(geom, blades, harmonic):
    angle = 2.0 * math.pi * jnp.arange(NS, dtype=jnp.float32) / NS
    src_x = cycle_radius * jnp.cos(angle)
    src_y = cycle_radius * jnp.sin(angle)
    dx = geom[0][:, None] - src_x[None, :]
    dy = geom[1][:, None] - src_y[None, :]
    dz = geom[2][:, None] - cycle_height
    r_sq = dx * dx + dy * dy + dz * dz
    g_re, g_im, f_re, f_im = green_parts(r_sq)
    normal_part = (
        dx * geom[3][:, None] + dy * geom[4][:, None] + dz * geom[5][:, None]
    ) / wavenumber
    h_re = g_re - f_im * normal_part
    h_im = g_im + f_re * normal_part
    modes = (blades * harmonic).astype(jnp.float32)
    e_re = jnp.cos(angle[:, None] * modes[None, :])
    e_im = jnp.sin(angle[:, None] * modes[None, :])
    high = lax.Precision.HIGHEST
    b_re = jnp.dot(h_re, e_re, precision=high) - jnp.dot(h_im, e_im, precision=high)
    b_im = jnp.dot(h_re, e_im, precision=high) + jnp.dot(h_im, e_re, precision=high)
    return jnp.concatenate([b_re, b_im], axis=1)


def correction(values, index_local, weights):
    count = index_local.shape[0]
    nvec = values.shape[1] // 2
    nearby = values[index_local]
    w_re = weights[:count][:, :, None]
    w_im = weights[count:][:, :, None]
    part_re = jnp.sum(w_re * nearby[:, :, :nvec] - w_im * nearby[:, :, nvec:], axis=0)
    part_im = jnp.sum(w_re * nearby[:, :, nvec:] + w_im * nearby[:, :, :nvec], axis=0)
    return jnp.concatenate([part_re, part_im], axis=1)


def local(krylov, geometry, corr_index, corr_weight, blades, harmonic, observer_angles):
    nrows = lax.axis_size("rows")
    ncols = lax.axis_size("cols")
    row_at = lax.axis_index("rows")
    col_at = lax.axis_index("cols")
    piece = krylov.shape[0]
    width = krylov.shape[1]
    panels = piece * nrows * ncols
    row_geom = collect(geometry, "cols", 1)
    col_geom = collect(geometry, "rows", 1)
    col_vectors = collect(krylov, "rows", 0)
    obs_each = observer_angles.shape[1] // (nrows * ncols)
    group = ncols * obs_each
    angles = lax.dynamic_slice_in_dim(observer_angles, row_at * group, group, 1)
    part, far_part = tile_products(
        row_geom, col_geom, col_vectors, angles, col_at * piece, row_at * piece, panels
    )
    applied = sent_and_summed(part, "cols", 0)
    first_panel = (row_at * ncols + col_at) * piece
    values = krylov.astype(jnp.float32)
    near = correction(values, corr_index - first_panel, corr_weight)
    source = incident(geometry, blades, harmonic)
    residual = source - (0.5 * values + near + applied)
    far_field = sent_and_summed(far_part, "cols", 0)
    return (residual, far_field)


def solution(mesh):
    placed = (
        P(("rows", "cols"), None),
        P(None, ("rows", "cols")),
        P(None, ("rows", "cols")),
        P(None, ("rows", "cols")),
        P(),
        P(),
        P(),
    )
    return jax.shard_map(
        local,
        mesh=mesh,
        in_specs=placed,
        out_specs=(P(("rows", "cols"), None), P(("rows", "cols"), None)),
        check_vma=False,
    )
```

```python
import functools
import math

import jax
import jax.numpy as jnp
from jax import lax
from jax.experimental import pallas as pl
from jax.experimental.pallas import tpu as pltpu
from jax.sharding import PartitionSpec as P

BF = jnp.bfloat16
F32 = jnp.float32
NS = 64
LANES = 128

wavenumber = 20.0
cycle_radius = 0.7
cycle_height = 1.0
four_pi = 4.0 * math.pi
two_pi = 2.0 * math.pi
kappa = wavenumber / two_pi

dot = functools.partial(jnp.dot, preferred_element_type=F32)


def pieces(x):
    first = x.astype(BF).astype(F32)
    rest = x - first
    second = rest.astype(BF).astype(F32)
    return first, second, (rest - second).astype(BF).astype(F32)


def left_stack(x):
    a, b, c = pieces(x)
    return jnp.concatenate([a, a, b, a, c, b], axis=0)


def right_stack(x):
    a, b, c = pieces(x)
    return jnp.concatenate([a, b, a, c, a, b], axis=0).astype(BF)


def panel_rows(g):
    row = lax.broadcasted_iota(jnp.int32, g.shape, 0)
    center = row < 3
    normal = pltpu.roll(g, 5, 0)
    c_sq = jnp.sum(jnp.where(center, g * g, 0.0), axis=0, keepdims=True)
    n_c = jnp.sum(jnp.where(center, g * normal, 0.0), axis=0, keepdims=True)
    return row, center, normal, c_sq, n_c, g[6:7]


def left_features(g, soft_sq):
    row, center, normal, c_sq, n_c, _ = panel_rows(g)
    size = (kappa * kappa) * (c_sq + soft_sq)
    one = jnp.where(row == 3, 1.0, jnp.where(row == 4, size, 0.0))
    two = jnp.where(row == 3, n_c, 0.0)
    return (
        left_stack(jnp.where(center, g, one)),
        left_stack(jnp.where(center, normal, two)),
    )


def right_features(g):
    row, center, normal, c_sq, n_c, area = panel_rows(g)
    scale = area * (kappa * kappa / four_pi)
    k_sq = kappa * kappa
    r_sq = jnp.where(
        center, -2.0 * k_sq * g, jnp.where(row == 3, k_sq * c_sq, jnp.where(row == 4, 1.0, 0.0))
    )
    along_col = jnp.where(
        center, -wavenumber * scale * normal, jnp.where(row == 3, wavenumber * scale * n_c, 0.0)
    )
    along_row = jnp.where(center, scale * g, jnp.where(row == 3, -scale, 0.0))
    far_turns = jnp.where(center, kappa * g, 0.0)
    far_scale = jnp.where(center, -wavenumber * area * normal, 0.0)
    return [right_stack(v) for v in (r_sq, along_col, along_row, far_turns, far_scale)]


def operator_tile(r_sq, along_col, along_row):
    inv = lax.rsqrt(r_sq)
    turns = r_sq * inv
    part = (turns - jnp.round(turns)).astype(BF)
    u = inv.astype(BF)
    a = along_col.astype(BF)
    b = along_row.astype(BF)

    def const(v):
        return jnp.asarray(v, BF)

    z = part * part
    sin_poly = (z * const(SIN[2]) + const(SIN[1])) * z + const(SIN[0])
    cos_poly = (z * const(COS[2]) + const(COS[1])) * z + const(COS[0])
    s = (part * u) * sin_poly
    c = u * cos_poly
    re = u * u - s * s
    im = s * c
    w = u * const(1.0 / two_pi)
    p = b - w * a
    q = a + w * b
    return re * p - im * q, re * q + im * p


root2 = math.sqrt(2.0)
SIN = [root2 * v for v in (3.14064003, -5.1369052, 2.29954689)]
COS = [root2 * v for v in (0.99940322, -4.89118661, 3.5838431)]


def far_values(turns, scale):
    part = turns - jnp.round(turns)
    z = part * part
    s = part * (((z * -0.55463616 + 2.54189901) * z + -5.16714279) * z + 3.14158202)
    c = ((z * -1.22212692 + 4.04128377) * z + -4.93393801) * z + 0.9999933
    s2 = s + s
    return (scale * (s2 * c)).astype(BF), (scale * (1.0 - s2 * s)).astype(BF)


def sin_cos(turns):
    part = turns - jnp.round(turns)
    quarter = jnp.round(4.0 * part)
    y = (part - 0.25 * quarter) * two_pi
    z = y * y
    s = y * (1.0 + z * (-1.0 / 6 + z * (1.0 / 120 + z * (-1.0 / 5040 + z * (1.0 / 362880)))))
    c = 1.0 + z * (-0.5 + z * (1.0 / 24 + z * (-1.0 / 720 + z * (1.0 / 40320))))
    odd = jnp.abs(quarter) == 1.0
    sin_v = jnp.where(odd, c, s)
    cos_v = jnp.where(odd, s, c)
    sin_v = jnp.where((quarter == -1.0) | (jnp.abs(quarter) == 2.0), -sin_v, sin_v)
    cos_v = jnp.where((quarter == 1.0) | (jnp.abs(quarter) == 2.0), -cos_v, cos_v)
    return sin_v, cos_v


ROWS = 512
COLS = 512
BLOCK = 256
MESH = pl.DeviceIdType.MESH


def turned(x):
    half = x.shape[1] // 2
    return jnp.concatenate([-x[:, half:], x[:, :half]], axis=1)


def incident(g, blades, harmonic):
    gt = g.T
    col = lambda i: gt[:, i : i + 1]
    source = lax.broadcasted_iota(jnp.int32, (1, NS), 1).astype(F32) * (1.0 / NS)
    sin_s, cos_s = sin_cos(source)
    dx = col(0) - cycle_radius * cos_s
    dy = col(1) - cycle_radius * sin_s
    dz = col(2) - cycle_height
    r_sq = dx * dx + dy * dy + dz * dz
    inv = lax.rsqrt(r_sq)
    sin_r, cos_r = sin_cos(r_sq * inv * kappa)
    g_re = cos_r * inv * (1.0 / four_pi)
    g_im = sin_r * inv * (1.0 / four_pi)
    f_re = (-g_re * inv - wavenumber * g_im) * inv
    f_im = (-g_im * inv + wavenumber * g_re) * inv
    along = (dx * col(3) + dy * col(4) + dz * col(5)) * (1.0 / wavenumber)
    h = jnp.concatenate([g_re - f_im * along, g_im + f_re * along], axis=1)
    modes = blades * harmonic
    at = lax.broadcasted_iota(jnp.int32, (NS, modes.shape[1]), 0)
    e_im, e_re = sin_cos(((at * modes) % NS).astype(F32) * (1.0 / NS))
    e = jnp.concatenate(
        [jnp.concatenate([e_re, e_im], axis=1), jnp.concatenate([-e_im, e_re], axis=1)], axis=0
    )
    return jnp.dot(h, e, precision=lax.Precision.HIGHEST, preferred_element_type=F32)


def correction(x, index, weight):
    count, n = index.shape
    both = jnp.concatenate([index.astype(F32), weight], axis=0).T
    lane = lax.broadcasted_iota(jnp.int32, (n, n), 1).astype(F32)
    w_re = jnp.zeros((n, n), F32)
    w_im = jnp.zeros((n, n), F32)
    for c in range(count):
        hit = lane == both[:, c : c + 1]
        w_re += jnp.where(hit, both[:, count + c : count + c + 1], 0.0)
        w_im += jnp.where(hit, both[:, 2 * count + c : 2 * count + c + 1], 0.0)
    x2 = jnp.concatenate([x, turned(x)], axis=0)
    total = jnp.zeros((n, x.shape[1]), F32)
    for part in pieces(jnp.concatenate([w_re, w_im], axis=1)):
        total += dot(part.astype(BF), x2)
    return total


def kernel(
    nrows, ncols,
    krylov, geometry, corr_index, corr_weight, blades, harmonic, angles,
    out, far_out,
    cgeo, rgeo, left_a, left_b, r0, r1, r2, r3, r4, x2, p0, p1, p2, p3, p4, p5, t0, t1, acc, base,
    stage, far_stage, part_in, far_in,
    send_sem, cgeo_sem, rgeo_sem, x_sem, far_sem, part_sem,
):
    rights = (r0, r1, r2, r3, r4)
    planes = ((p0, p1, p2), (p3, p4, p5))
    tiles = (t0, t1)
    r = lax.axis_index("rows")
    c = lax.axis_index("cols")
    core = r % 2
    chip = r // 2
    chips = nrows // 2
    sibling = r + 1 - 2 * core
    n_cols = nrows * BLOCK
    n_rows = ncols * BLOCK
    n_obs = far_stage.shape[0]
    obs = n_obs // ncols
    steps = n_cols // COLS
    half = COLS // LANES
    panels = nrows * ncols * BLOCK
    sends = []

    def send(src, dst, sem, row, col):
        copy = pltpu.make_async_remote_copy(
            src_ref=src, dst_ref=dst, send_sem=send_sem.at[len(sends)], recv_sem=sem,
            device_id=(row, col), device_id_type=MESH,
        )
        copy.start()
        sends.append(copy)

    def arrived(dst, sem):
        pltpu.make_async_remote_copy(
            src_ref=dst, dst_ref=dst, send_sem=send_sem.at[0], recv_sem=sem,
            device_id=(r, c), device_id_type=MESH,
        ).wait_recv()

    barrier = pltpu.get_barrier_semaphore()
    for k in range(1, nrows):
        pl.semaphore_signal(barrier, inc=1, device_id=((r + k) % nrows, c), device_id_type=MESH)
    for k in range(1, ncols):
        pl.semaphore_signal(barrier, inc=1, device_id=(r, (c + k) % ncols), device_id_type=MESH)

    ang = angles[:, pl.ds(pl.multiple_of(r * n_obs, n_obs), n_obs)] * (1.0 / two_pi)
    sin_t, cos_t = sin_cos(ang[0:1])
    sin_p, cos_p = sin_cos(ang[1:2])
    e = jnp.concatenate([sin_t * cos_p, sin_t * sin_p, cos_t, jnp.zeros((5, n_obs), F32)], axis=0)
    left_a[pl.ds(n_rows, n_obs), :] = left_stack(e).T.astype(BF)
    cgeo[chip] = geometry[...]
    rgeo[c] = geometry[...]
    x2[chip // 2, chip % 2] = krylov[...]

    pl.semaphore_wait(barrier, nrows + ncols - 2)
    for k in range(1, nrows):
        peer = (r + k) % nrows
        at = (r + peer) % 2 * chips + chip
        send(geometry, cgeo.at[at], cgeo_sem.at[at], peer, c)
    for k in range(1, ncols):
        send(geometry, rgeo.at[c], rgeo_sem.at[c], r, (c + k) % ncols)
    send(krylov, x2.at[(chips + chip) // 2, chip % 2], x_sem.at[chips + chip], sibling, c)
    for k in range(1, chips):
        peer = (chip + k) % chips * 2 + core
        send(krylov, x2.at[chip // 2, chip % 2], x_sem.at[chip], peer, c)

    own = jnp.concatenate([geometry[...], jnp.zeros((1, BLOCK), F32)], axis=0)
    x = krylov[...]
    index = corr_index[...] - (r * ncols + c) * BLOCK
    base[...] = (
        incident(own, blades[...], harmonic[...])
        - 0.5 * x.astype(F32)
        - correction(x, index, corr_weight[...])
    )

    for k in range(1, nrows):
        at = (chip + k) % nrows
        arrived(cgeo.at[at], cgeo_sem.at[at])
    g = jnp.concatenate([cgeo[i] for i in range(nrows)], axis=1)
    g = jnp.concatenate([g, jnp.zeros((1, n_cols), F32)], axis=0)
    for ref, v in zip(rights, right_features(g)):
        ref[...] = v
    for k in range(1, ncols):
        at = (c + k) % ncols
        arrived(rgeo.at[at], rgeo_sem.at[at])
    g = jnp.concatenate([rgeo[i] for i in range(ncols)], axis=1)
    g = jnp.concatenate([g, jnp.zeros((1, n_rows), F32)], axis=0)
    la, lb = left_features(g, 4.0 / panels)
    left_a[pl.ds(0, n_rows), :] = la.T.astype(BF)
    left_b[...] = lb.T.astype(BF)

    def make_geometry(first, step, far, into):
        cols = pl.ds(pl.multiple_of(step * COLS, COLS), COLS)
        rows = pl.ds(pl.multiple_of(first, ROWS), ROWS)
        la = left_a[rows, :]
        if far:
            into[0][...] = dot(la, rights[3][:, cols])
            into[1][...] = dot(la, rights[4][:, cols])
        else:
            into[0][...] = dot(la, rights[0][:, cols])
            into[1][...] = dot(la, rights[1][:, cols])
            into[2][...] = dot(left_b[rows, :], rights[2][:, cols])

    def make_values(step, far, frm, tile):
        if far:
            re, im = far_values(frm[0][...], frm[1][...])
        else:
            re, im = operator_tile(frm[0][...], frm[1][...], frm[2][...])
        for h in range(half):
            tile[step * 2 * half + h] = re[:, h * LANES : (h + 1) * LANES]
            tile[step * 2 * half + half + h] = im[:, h * LANES : (h + 1) * LANES]

    def product(step, tile, rows):
        lhs = jnp.concatenate([tile[step * 2 * half + h, rows, :] for h in range(2 * half)], axis=1)
        return dot(lhs, x2[step].reshape(2 * COLS, x2.shape[-1]))

    every = pl.ds(0, ROWS)
    blocks = n_rows // ROWS
    where = [(c // 2 + 1 + b) % blocks for b in range(blocks)]
    seq = [(n_rows, True)] + [(w * ROWS, False) for w in where]

    def run(ph, first_h, last_h, prepare):
        gen, mul = ph < len(seq), ph > 0

        @pl.loop(first_h, last_h)
        def _(h):
            for par in range(2):
                step = 2 * h + par
                if gen:
                    first, far = seq[ph]
                    make_geometry(first, lax.rem(step + 1, steps), far, planes[1 - par])
                    make_values(step, far, planes[par], tiles[ph % 2])
                if mul:
                    if prepare:
                        for b in range(2):
                            if prepare > 1:
                                arrived(x2.at[step, b], x_sem.at[2 * step + b])
                            x2[step, 2 + b] = turned(x2[step, b])
                    acc[...] += product(step, tiles[(ph - 1) % 2], every)

    def send_parts(block):
        for b in range(2):
            owner = where[block] * 2 + b
            send(stage.at[owner], part_in.at[c], part_sem.at[c], r, owner)

    for ph in range(len(seq)):
        first, far = seq[ph]
        make_geometry(first, 0, far, planes[0])
        if ph > 0:
            acc[...] = jnp.zeros_like(acc)
        if ph == 2:
            for k in range(1, ncols):
                owner = (c + k) % ncols
                rows = pl.ds(pl.multiple_of(owner * obs, obs), obs)
                send(far_stage.at[rows, :], far_in.at[c], far_sem.at[c], r, owner)
        if ph > 2:
            send_parts(ph - 3)
        if ph == 1:
            run(ph, 0, steps // 4, 1)
            run(ph, steps // 4, steps // 2, 2)
        else:
            run(ph, 0, steps // 2, 0)
        if ph == 0:
            for k in range(1, chips):
                at = (chip + k) % chips
                here = x2.at[at // 2, at % 2]
                arrived(here, x_sem.at[at])
                send(here, x2.at[(chips + at) // 2, at % 2], x_sem.at[chips + at], sibling, c)
        elif ph == 1:
            far_stage[...] = acc[...]
        else:
            for b in range(2):
                stage[where[ph - 2] * 2 + b] = acc[pl.ds(b * BLOCK, BLOCK), :].astype(BF)

    tile = tiles[(len(seq) - 1) % 2]
    same = lax.broadcasted_iota(jnp.int32, (BLOCK, LANES), 0)
    lane = lax.broadcasted_iota(jnp.int32, (BLOCK, LANES), 1)
    rows = pl.ds(pl.multiple_of(c % 2 * BLOCK, BLOCK), BLOCK)
    for h in range(BLOCK // LANES):
        for part in range(2):
            at = chip // 2 * 2 * half + part * half + chip % 2 * (BLOCK // LANES) + h
            v = tile[at, rows, :].astype(F32)
            tile[at, rows, :] = jnp.where(same == lane + h * LANES, 0.0, v).astype(BF)

    send_parts(blocks - 2)
    partner = c + 1 - 2 * (c % 2)
    mine = acc.at[pl.ds(0, BLOCK), :]
    theirs = acc.at[pl.ds(BLOCK, BLOCK), :]
    other_rows = pl.ds(pl.multiple_of((1 - c % 2) * BLOCK, BLOCK), BLOCK)
    theirs[...] = product(0, tile, other_rows)

    @pl.loop(1, steps)
    def _(step):
        theirs[...] += product(step, tile, other_rows)

    stage[partner] = theirs[...].astype(BF)
    mine[...] = product(0, tile, rows)
    send(stage.at[partner], part_in.at[c], part_sem.at[c], r, partner)

    @pl.loop(1, steps)
    def _(step):
        mine[...] += product(step, tile, rows)

    total = far_stage[pl.ds(pl.multiple_of(c * obs, obs), obs), :]
    for k in range(1, ncols):
        at = (c + k) % ncols
        arrived(far_in.at[at], far_sem.at[at])
        total += far_in[at]
    far_out[...] = total
    total = base[...] - mine[...]
    for k in range(1, ncols):
        at = (c + k) % ncols
        arrived(part_in.at[at], part_sem.at[at])
        total -= part_in[at].astype(F32)
    out[...] = total
    for copy in sends:
        copy.wait_send()


def local(krylov, geometry, corr_index, corr_weight, blades, harmonic, observer_angles):
    nrows = lax.axis_size("rows")
    ncols = lax.axis_size("cols")
    width = krylov.shape[1]
    n_cols, n_rows = nrows * BLOCK, ncols * BLOCK
    n_obs = observer_angles.shape[1] // nrows
    n_sends = (nrows - 1) + 4 * (ncols - 1) + nrows
    vm = pl.BlockSpec(memory_space=pltpu.VMEM)
    dma = pltpu.SemaphoreType.DMA
    return pl.pallas_call(
        functools.partial(kernel, nrows, ncols),
        out_shape=(
            jax.ShapeDtypeStruct((BLOCK, width), F32),
            jax.ShapeDtypeStruct((n_obs // ncols, width), F32),
        ),
        in_specs=[vm] * 7,
        out_specs=(vm, vm),
        scratch_shapes=[
            pltpu.VMEM((nrows, 7, BLOCK), F32),
            pltpu.VMEM((ncols, 7, BLOCK), F32),
            pltpu.VMEM((n_rows + n_obs, 48), BF),
            pltpu.VMEM((n_rows, 48), BF),
        ]
        + [pltpu.VMEM((48, n_cols), BF)] * 5
        + [pltpu.VMEM((n_cols // COLS, 4, BLOCK, width), BF)]
        + [pltpu.VMEM((ROWS, COLS), F32)] * 6
        + [pltpu.VMEM((2 * n_cols // LANES, ROWS, LANES), BF)] * 2
        + [
            pltpu.VMEM((ROWS, width), F32),
            pltpu.VMEM((BLOCK, width), F32),
            pltpu.VMEM((ncols, BLOCK, width), BF),
            pltpu.VMEM((n_obs, width), F32),
            pltpu.VMEM((ncols, BLOCK, width), BF),
            pltpu.VMEM((ncols, n_obs // ncols, width), F32),
            dma((n_sends,)),
            dma((nrows,)),
            dma((ncols,)),
            dma((nrows,)),
            dma((ncols,)),
            dma((ncols,)),
        ],
        compiler_params=pltpu.CompilerParams(
            collective_id=0, has_side_effects=True, vmem_limit_bytes=60 << 20
        ),
        name="burton_miller",
    )(krylov, geometry, corr_index, corr_weight, blades[None], harmonic[None], observer_angles)


def solution(mesh):
    placed = (
        P(("rows", "cols"), None),
        P(None, ("rows", "cols")),
        P(None, ("rows", "cols")),
        P(None, ("rows", "cols")),
        P(),
        P(),
        P(),
    )
    return jax.shard_map(
        local,
        mesh=mesh,
        in_specs=placed,
        out_specs=(P(("rows", "cols"), None), P(("rows", "cols"), None)),
        check_vma=False,
    )
```

```python
import functools
import math

import jax
import jax.numpy as jnp
from jax import lax
from jax.experimental import pallas as pl
from jax.experimental.pallas import tpu as pltpu
from jax.sharding import PartitionSpec as P

BF = jnp.bfloat16
F32 = jnp.float32
NS = 64
LANES = 128

wavenumber = 20.0
cycle_radius = 0.7
cycle_height = 1.0
four_pi = 4.0 * math.pi
two_pi = 2.0 * math.pi
kappa = wavenumber / two_pi

dot = functools.partial(jnp.dot, preferred_element_type=F32)


def pieces(x):
    first = x.astype(BF).astype(F32)
    rest = x - first
    second = rest.astype(BF).astype(F32)
    return first, second, (rest - second).astype(BF).astype(F32)


def left_stack(x):
    a, b, c = pieces(x)
    return jnp.concatenate([a, a, b, a, c, b], axis=0)


def right_stack(x):
    a, b, c = pieces(x)
    return jnp.concatenate([a, b, a, c, a, b], axis=0).astype(BF)


def panel_rows(g):
    row = lax.broadcasted_iota(jnp.int32, g.shape, 0)
    center = row < 3
    normal = pltpu.roll(g, 5, 0)
    c_sq = jnp.sum(jnp.where(center, g * g, 0.0), axis=0, keepdims=True)
    n_c = jnp.sum(jnp.where(center, g * normal, 0.0), axis=0, keepdims=True)
    return row, center, normal, c_sq, n_c, g[6:7]


def left_features(g, soft_sq):
    row, center, normal, c_sq, n_c, _ = panel_rows(g)
    size = (kappa * kappa) * (c_sq + soft_sq)
    one = jnp.where(row == 3, 1.0, jnp.where(row == 4, size, 0.0))
    two = jnp.where(row == 3, n_c, 0.0)
    return (
        left_stack(jnp.where(center, g, one)),
        left_stack(jnp.where(center, normal, two)),
    )


def right_features(g):
    row, center, normal, c_sq, n_c, area = panel_rows(g)
    scale = area * (kappa * kappa / four_pi)
    k_sq = kappa * kappa
    r_sq = jnp.where(
        center, -2.0 * k_sq * g, jnp.where(row == 3, k_sq * c_sq, jnp.where(row == 4, 1.0, 0.0))
    )
    along_col = jnp.where(
        center, -wavenumber * scale * normal, jnp.where(row == 3, wavenumber * scale * n_c, 0.0)
    )
    along_row = jnp.where(center, scale * g, jnp.where(row == 3, -scale, 0.0))
    far_turns = jnp.where(center, kappa * g, 0.0)
    far_scale = jnp.where(center, -wavenumber * area * normal, 0.0)
    return [right_stack(v) for v in (r_sq, along_col, along_row, far_turns, far_scale)]


def operator_tile(r_sq, along_col, along_row):
    inv = lax.rsqrt(r_sq)
    turns = r_sq * inv
    part = (turns - jnp.round(turns)).astype(BF)
    u = inv.astype(BF)
    a = along_col.astype(BF)
    b = along_row.astype(BF)

    def const(v):
        return jnp.asarray(v, BF)

    z = part * part
    sin_poly = (z * const(SIN[2]) + const(SIN[1])) * z + const(SIN[0])
    cos_poly = (z * const(COS[2]) + const(COS[1])) * z + const(COS[0])
    s = (part * u) * sin_poly
    c = u * cos_poly
    re = u * u - s * s
    im = s * c
    w = u * const(1.0 / two_pi)
    p = b - w * a
    q = a + w * b
    return re * p - im * q, re * q + im * p


root2 = math.sqrt(2.0)
SIN = [root2 * v for v in (3.14064003, -5.1369052, 2.29954689)]
COS = [root2 * v for v in (0.99940322, -4.89118661, 3.5838431)]


def far_values(turns, scale):
    part = turns - jnp.round(turns)
    z = part * part
    s = part * (((z * -0.55463616 + 2.54189901) * z + -5.16714279) * z + 3.14158202)
    c = ((z * -1.22212692 + 4.04128377) * z + -4.93393801) * z + 0.9999933
    s2 = s + s
    return (scale * (s2 * c)).astype(BF), (scale * (1.0 - s2 * s)).astype(BF)


def sin_cos(turns):
    part = turns - jnp.round(turns)
    quarter = jnp.round(4.0 * part)
    y = (part - 0.25 * quarter) * two_pi
    z = y * y
    s = y * (1.0 + z * (-1.0 / 6 + z * (1.0 / 120 + z * (-1.0 / 5040 + z * (1.0 / 362880)))))
    c = 1.0 + z * (-0.5 + z * (1.0 / 24 + z * (-1.0 / 720 + z * (1.0 / 40320))))
    odd = jnp.abs(quarter) == 1.0
    sin_v = jnp.where(odd, c, s)
    cos_v = jnp.where(odd, s, c)
    sin_v = jnp.where((quarter == -1.0) | (jnp.abs(quarter) == 2.0), -sin_v, sin_v)
    cos_v = jnp.where((quarter == 1.0) | (jnp.abs(quarter) == 2.0), -cos_v, cos_v)
    return sin_v, cos_v


ROWS = 512
COLS = 512
BLOCK = 256
MESH = pl.DeviceIdType.MESH


def turned(x):
    half = x.shape[1] // 2
    return jnp.concatenate([-x[:, half:], x[:, :half]], axis=1)


def incident(g, blades, harmonic):
    gt = g.T
    col = lambda i: gt[:, i : i + 1]
    source = lax.broadcasted_iota(jnp.int32, (1, NS), 1).astype(F32) * (1.0 / NS)
    sin_s, cos_s = sin_cos(source)
    dx = col(0) - cycle_radius * cos_s
    dy = col(1) - cycle_radius * sin_s
    dz = col(2) - cycle_height
    r_sq = dx * dx + dy * dy + dz * dz
    inv = lax.rsqrt(r_sq)
    sin_r, cos_r = sin_cos(r_sq * inv * kappa)
    g_re = cos_r * inv * (1.0 / four_pi)
    g_im = sin_r * inv * (1.0 / four_pi)
    f_re = (-g_re * inv - wavenumber * g_im) * inv
    f_im = (-g_im * inv + wavenumber * g_re) * inv
    along = (dx * col(3) + dy * col(4) + dz * col(5)) * (1.0 / wavenumber)
    h = jnp.concatenate([g_re - f_im * along, g_im + f_re * along], axis=1)
    modes = blades * harmonic
    at = lax.broadcasted_iota(jnp.int32, (NS, modes.shape[1]), 0)
    e_im, e_re = sin_cos(((at * modes) % NS).astype(F32) * (1.0 / NS))
    e = jnp.concatenate(
        [jnp.concatenate([e_re, e_im], axis=1), jnp.concatenate([-e_im, e_re], axis=1)], axis=0
    )
    return jnp.dot(h, e, precision=lax.Precision.HIGHEST, preferred_element_type=F32)


def correction(x, index, weight):
    count, n = index.shape
    both = jnp.concatenate([index.astype(F32), weight], axis=0).T
    lane = lax.broadcasted_iota(jnp.int32, (n, n), 1).astype(F32)
    w_re = jnp.zeros((n, n), F32)
    w_im = jnp.zeros((n, n), F32)
    for c in range(count):
        hit = lane == both[:, c : c + 1]
        w_re += jnp.where(hit, both[:, count + c : count + c + 1], 0.0)
        w_im += jnp.where(hit, both[:, 2 * count + c : 2 * count + c + 1], 0.0)
    x2 = jnp.concatenate([x, turned(x)], axis=0)
    total = jnp.zeros((n, x.shape[1]), F32)
    for part in pieces(jnp.concatenate([w_re, w_im], axis=1)):
        total += dot(part.astype(BF), x2)
    return total


def kernel(
    nrows, ncols, left_a, left_b, r0, r1, r2, r3, r4, t0, t1, t2,
    krylov, geometry, corr_index, corr_weight, blades, harmonic, angles,
    out, far_out,
    cgeo, rgeo, x2, p0, p1, p2, p3, p4, p5, acc, base,
    stage, far_stage, part_in, far_in,
    send_sem, cgeo_sem, rgeo_sem, x_sem, far_sem, part_sem,
):
    rights = (r0, r1, r2, r3, r4)
    planes = ((p0, p1, p2), (p3, p4, p5))
    tiles = (t0, t1, t2)
    r = lax.axis_index("rows")
    c = lax.axis_index("cols")
    core = r % 2
    chip = r // 2
    chips = nrows // 2
    sibling = r + 1 - 2 * core
    n_cols = nrows * BLOCK
    n_rows = ncols * BLOCK
    n_obs = far_stage.shape[0]
    obs = n_obs // ncols
    steps = n_cols // COLS
    half = COLS // LANES
    panels = nrows * ncols * BLOCK
    sends = []
    first_forward = (nrows - 1) + 3 * (ncols - 1) + chips

    def send(src, dst, sem, row, col):
        copy = pltpu.make_async_remote_copy(
            src_ref=src, dst_ref=dst, send_sem=send_sem.at[len(sends)], recv_sem=sem,
            device_id=(row, col), device_id_type=MESH,
        )
        copy.start()
        sends.append(copy)

    def forward(k, at):
        return pltpu.make_async_remote_copy(
            src_ref=x2.at[at // 2, at % 2], dst_ref=x2.at[(chips + at) // 2, at % 2],
            send_sem=send_sem.at[first_forward + k - 1], recv_sem=x_sem.at[chips + at],
            device_id=(sibling, c), device_id_type=MESH,
        )

    def arrived(dst, sem):
        pltpu.make_async_remote_copy(
            src_ref=dst, dst_ref=dst, send_sem=send_sem.at[0], recv_sem=sem,
            device_id=(r, c), device_id_type=MESH,
        ).wait_recv()

    barrier = pltpu.get_barrier_semaphore()
    for k in range(1, nrows):
        pl.semaphore_signal(barrier, inc=1, device_id=((r + k) % nrows, c), device_id_type=MESH)
    for k in range(1, ncols):
        pl.semaphore_signal(barrier, inc=1, device_id=(r, (c + k) % ncols), device_id_type=MESH)

    ang = angles[:, pl.ds(pl.multiple_of(r * n_obs, n_obs), n_obs)] * (1.0 / two_pi)
    sin_t, cos_t = sin_cos(ang[0:1])
    sin_p, cos_p = sin_cos(ang[1:2])
    e = jnp.concatenate([sin_t * cos_p, sin_t * sin_p, cos_t, jnp.zeros((5, n_obs), F32)], axis=0)
    left_a[pl.ds(n_rows, n_obs), :] = left_stack(e).T.astype(BF)
    cgeo[chip] = geometry[...]
    rgeo[c] = geometry[...]
    x2[chip // 2, chip % 2] = krylov[...]

    x = krylov[...]
    index = corr_index[...] - (r * ncols + c) * BLOCK
    base[...] = -0.5 * x.astype(F32) - correction(x, index, corr_weight[...])

    pl.semaphore_wait(barrier, nrows + ncols - 2)
    for k in range(1, nrows):
        peer = (r + k) % nrows
        at = (r + peer) % 2 * chips + chip
        send(geometry, cgeo.at[at], cgeo_sem.at[at], peer, c)
    for k in range(1, ncols):
        send(geometry, rgeo.at[c], rgeo_sem.at[c], r, (c + k) % ncols)
    send(krylov, x2.at[(chips + chip) // 2, chip % 2], x_sem.at[chips + chip], sibling, c)
    for k in range(1, chips):
        peer = (chip + k) % chips * 2 + core
        send(krylov, x2.at[chip // 2, chip % 2], x_sem.at[chip], peer, c)

    own = jnp.concatenate([geometry[...], jnp.zeros((1, BLOCK), F32)], axis=0)
    base[...] += incident(own, blades[...], harmonic[...])

    for k in range(1, nrows):
        at = (chip + k) % nrows
        arrived(cgeo.at[at], cgeo_sem.at[at])
    g = jnp.concatenate([cgeo[i] for i in range(nrows)], axis=1)
    g = jnp.concatenate([g, jnp.zeros((1, n_cols), F32)], axis=0)
    for ref, v in zip(rights, right_features(g)):
        ref[...] = v
    for k in range(1, ncols):
        at = (c + k) % ncols
        arrived(rgeo.at[at], rgeo_sem.at[at])
    g = jnp.concatenate([rgeo[i] for i in range(ncols)], axis=1)
    g = jnp.concatenate([g, jnp.zeros((1, n_rows), F32)], axis=0)
    la, lb = left_features(g, 4.0 / panels)
    left_a[pl.ds(0, n_rows), :] = la.T.astype(BF)
    left_b[...] = lb.T.astype(BF)

    def make_geometry(first, step, far, into):
        cols = pl.ds(pl.multiple_of(step * COLS, COLS), COLS)
        rows = pl.ds(pl.multiple_of(first, ROWS), ROWS)
        la = left_a[rows, :]
        if far:
            into[0][...] = dot(la, rights[3][:, cols])
            into[1][...] = dot(la, rights[4][:, cols])
        else:
            into[0][...] = dot(la, rights[0][:, cols])
            into[1][...] = dot(la, rights[1][:, cols])
            into[2][...] = dot(left_b[rows, :], rights[2][:, cols])

    def make_values(step, far, frm, tile):
        if far:
            re, im = far_values(frm[0][...], frm[1][...])
        else:
            re, im = operator_tile(frm[0][...], frm[1][...], frm[2][...])
        for h in range(half):
            tile[step * 2 * half + h] = re[:, h * LANES : (h + 1) * LANES]
            tile[step * 2 * half + half + h] = im[:, h * LANES : (h + 1) * LANES]

    def product(step, tile, rows):
        lhs = jnp.concatenate([tile[step * 2 * half + h, rows, :] for h in range(2 * half)], axis=1)
        return dot(lhs, x2[step].reshape(2 * COLS, x2.shape[-1]))

    every = pl.ds(0, ROWS)
    blocks = n_rows // ROWS
    where = [(c // 2 + 1 + b) % blocks for b in range(blocks)]
    seq = [(n_rows, True)] + [(w * ROWS, False) for w in where]
    lag = 2

    def prepare(step):
        for b in range(2):
            x2[step, 2 + b] = turned(x2[step, b])

    def run(ph, first_h, last_h, extra=None):
        gen, mul = ph < len(seq), ph >= lag

        @pl.loop(first_h, last_h)
        def _(h):
            for par in range(2):
                step = 2 * h + par
                if gen:
                    first, far = seq[ph]
                    make_geometry(first, lax.rem(step + 1, steps), far, planes[1 - par])
                    make_values(step, far, planes[par], tiles[ph % 3])
                if extra is not None:
                    extra(step)
                if mul:
                    acc[...] += product(step, tiles[(ph - lag) % 3], every)

    def pass_on(step):
        @pl.when(step > 0)
        def _():
            at = (chip + chips - step) % chips
            arrived(x2.at[at // 2, at % 2], x_sem.at[at])
            forward(step, at).start()

    def wait_and_prepare(step):
        for b in range(2):
            arrived(x2.at[step, b], x_sem.at[2 * step + b])
        prepare(step)

    def send_parts(block):
        for b in range(2):
            owner = where[block] * 2 + b
            send(stage.at[owner], part_in.at[c], part_sem.at[c], r, owner)

    for ph in range(len(seq) + 1):
        if ph < len(seq):
            first, far = seq[ph]
            make_geometry(first, 0, far, planes[0])
        if ph >= lag:
            acc[...] = jnp.zeros_like(acc)
        if ph == 3:
            for k in range(1, ncols):
                owner = (c + k) % ncols
                rows = pl.ds(pl.multiple_of(owner * obs, obs), obs)
                send(far_stage.at[rows, :], far_in.at[c], far_sem.at[c], r, owner)
        if ph > 3:
            send_parts(ph - 4)
        if ph == 1:
            run(ph, 0, steps // 2, pass_on)
        elif ph == 2:
            run(ph, 0, steps // 4, prepare)
            run(ph, steps // 4, steps // 2, wait_and_prepare)
        else:
            run(ph, 0, steps // 2)
        if ph == 2:
            far_stage[...] = acc[...]
        elif ph > 2:
            for b in range(2):
                stage[where[ph - 3] * 2 + b] = acc[pl.ds(b * BLOCK, BLOCK), :].astype(BF)

    tile = tiles[(len(seq) - 1) % 3]
    same = lax.broadcasted_iota(jnp.int32, (BLOCK, LANES), 0)
    lane = lax.broadcasted_iota(jnp.int32, (BLOCK, LANES), 1)
    rows = pl.ds(pl.multiple_of(c % 2 * BLOCK, BLOCK), BLOCK)
    for h in range(BLOCK // LANES):
        for part in range(2):
            at = chip // 2 * 2 * half + part * half + chip % 2 * (BLOCK // LANES) + h
            v = tile[at, rows, :].astype(F32)
            tile[at, rows, :] = jnp.where(same == lane + h * LANES, 0.0, v).astype(BF)

    send_parts(blocks - 2)
    partner = c + 1 - 2 * (c % 2)
    mine = acc.at[pl.ds(0, BLOCK), :]
    theirs = acc.at[pl.ds(BLOCK, BLOCK), :]
    other_rows = pl.ds(pl.multiple_of((1 - c % 2) * BLOCK, BLOCK), BLOCK)
    theirs[...] = product(0, tile, other_rows)

    @pl.loop(1, steps)
    def _(step):
        theirs[...] += product(step, tile, other_rows)

    stage[partner] = theirs[...].astype(BF)
    mine[...] = product(0, tile, rows)
    send(stage.at[partner], part_in.at[c], part_sem.at[c], r, partner)

    @pl.loop(1, steps)
    def _(step):
        mine[...] += product(step, tile, rows)

    total = far_stage[pl.ds(pl.multiple_of(c * obs, obs), obs), :]
    for k in range(1, ncols):
        at = (c + ncols - k) % ncols
        arrived(far_in.at[at], far_sem.at[at])
        total += far_in[at]
    far_out[...] = total
    total = base[...] - mine[...]
    for k in range(1, ncols):
        at = (c + ncols - k) % ncols
        arrived(part_in.at[at], part_sem.at[at])
        total -= part_in[at].astype(F32)
    out[...] = total
    for copy in sends:
        copy.wait_send()
    for k in range(1, chips):
        forward(k, (chip + chips - k) % chips).wait_send()


def local(krylov, geometry, corr_index, corr_weight, blades, harmonic, observer_angles):
    nrows = lax.axis_size("rows")
    ncols = lax.axis_size("cols")
    width = krylov.shape[1]
    n_cols, n_rows = nrows * BLOCK, ncols * BLOCK
    n_obs = observer_angles.shape[1] // nrows
    n_sends = (nrows - 1) + 4 * (ncols - 1) + nrows
    scoped = (
        [pltpu.VMEM((n_rows + n_obs, 48), BF), pltpu.VMEM((n_rows, 48), BF)]
        + [pltpu.VMEM((48, n_cols), BF)] * 5
        + [pltpu.VMEM((2 * n_cols // LANES, ROWS, LANES), BF)] * 3
    )

    def body(*refs):
        pl.run_scoped(lambda *own: kernel(nrows, ncols, *own, *refs), *scoped)

    vm = pl.BlockSpec(memory_space=pltpu.VMEM)
    dma = pltpu.SemaphoreType.DMA
    return pl.pallas_call(
        body,
        out_shape=(
            jax.ShapeDtypeStruct((BLOCK, width), F32),
            jax.ShapeDtypeStruct((n_obs // ncols, width), F32),
        ),
        in_specs=[vm] * 7,
        out_specs=(vm, vm),
        scratch_shapes=[
            pltpu.VMEM((nrows, 7, BLOCK), F32),
            pltpu.VMEM((ncols, 7, BLOCK), F32),
        ]
        + [pltpu.VMEM((n_cols // COLS, 4, BLOCK, width), BF)]
        + [pltpu.VMEM((ROWS, COLS), F32)] * 6
        + [
            pltpu.VMEM((ROWS, width), F32),
            pltpu.VMEM((BLOCK, width), F32),
            pltpu.VMEM((ncols, BLOCK, width), BF),
            pltpu.VMEM((n_obs, width), F32),
            pltpu.VMEM((ncols, BLOCK, width), BF),
            pltpu.VMEM((ncols, n_obs // ncols, width), F32),
            dma((n_sends,)),
            dma((nrows,)),
            dma((ncols,)),
            dma((nrows,)),
            dma((ncols,)),
            dma((ncols,)),
        ],
        compiler_params=pltpu.CompilerParams(
            collective_id=0, has_side_effects=True, vmem_limit_bytes=60 << 20
        ),
        name="burton_miller",
    )(krylov, geometry, corr_index, corr_weight, blades[None], harmonic[None], observer_angles)


def solution(mesh):
    placed = (
        P(("rows", "cols"), None),
        P(None, ("rows", "cols")),
        P(None, ("rows", "cols")),
        P(None, ("rows", "cols")),
        P(),
        P(),
        P(),
    )
    return jax.shard_map(
        local,
        mesh=mesh,
        in_specs=placed,
        out_specs=(P(("rows", "cols"), None), P(("rows", "cols"), None)),
        check_vma=False,
    )
```

```python
import functools
import math

import jax
import jax.numpy as jnp
from jax import lax
from jax.experimental import pallas as pl
from jax.experimental.pallas import tpu as pltpu
from jax.sharding import PartitionSpec as P

BF = jnp.bfloat16
F32 = jnp.float32
NS = 64
LANES = 128

wavenumber = 20.0
cycle_radius = 0.7
cycle_height = 1.0
four_pi = 4.0 * math.pi
two_pi = 2.0 * math.pi
kappa = wavenumber / two_pi

dot = functools.partial(jnp.dot, preferred_element_type=F32)


def pieces(x):
    first = x.astype(BF).astype(F32)
    rest = x - first
    second = rest.astype(BF).astype(F32)
    return first, second, (rest - second).astype(BF).astype(F32)


def left_stack(x):
    a, b, c = pieces(x)
    return jnp.concatenate([a, a, b, a, c, b], axis=0)


def right_stack(x):
    a, b, c = pieces(x)
    return jnp.concatenate([a, b, a, c, a, b], axis=0).astype(BF)


def panel_rows(g):
    row = lax.broadcasted_iota(jnp.int32, g.shape, 0)
    center = row < 3
    normal = pltpu.roll(g, 5, 0)
    c_sq = jnp.sum(jnp.where(center, g * g, 0.0), axis=0, keepdims=True)
    n_c = jnp.sum(jnp.where(center, g * normal, 0.0), axis=0, keepdims=True)
    return row, center, normal, c_sq, n_c, g[6:7]


def left_features(g, soft_sq):
    row, center, normal, c_sq, n_c, _ = panel_rows(g)
    size = (kappa * kappa) * (c_sq + soft_sq)
    one = jnp.where(row == 3, 1.0, jnp.where(row == 4, size, 0.0))
    two = jnp.where(row == 3, n_c, 0.0)
    return (
        left_stack(jnp.where(center, g, one)),
        left_stack(jnp.where(center, normal, two)),
    )


def right_features(g):
    row, center, normal, c_sq, n_c, area = panel_rows(g)
    scale = area * (kappa * kappa / four_pi)
    k_sq = kappa * kappa
    r_sq = jnp.where(
        center, -2.0 * k_sq * g, jnp.where(row == 3, k_sq * c_sq, jnp.where(row == 4, 1.0, 0.0))
    )
    along_col = jnp.where(
        center, -wavenumber * scale * normal, jnp.where(row == 3, wavenumber * scale * n_c, 0.0)
    )
    along_row = jnp.where(center, scale * g, jnp.where(row == 3, -scale, 0.0))
    far_turns = jnp.where(center, kappa * g, 0.0)
    far_scale = jnp.where(center, -wavenumber * area * normal, 0.0)
    return [right_stack(v) for v in (r_sq, along_col, along_row, far_turns, far_scale)]


def operator_tile(r_sq, along_col, along_row):
    inv = lax.rsqrt(r_sq)
    turns = r_sq * inv
    part = (turns - jnp.round(turns)).astype(BF)
    u = inv.astype(BF)
    a = along_col.astype(BF)
    b = along_row.astype(BF)

    def const(v):
        return jnp.asarray(v, BF)

    z = part * part
    sin_poly = (z * const(SIN[2]) + const(SIN[1])) * z + const(SIN[0])
    cos_poly = (z * const(COS[2]) + const(COS[1])) * z + const(COS[0])
    s = (part * u) * sin_poly
    c = u * cos_poly
    re = u * u - s * s
    im = s * c
    w = u * const(1.0 / two_pi)
    p = b - w * a
    q = a + w * b
    return re * p - im * q, re * q + im * p


root2 = math.sqrt(2.0)
SIN = [root2 * v for v in (3.14064003, -5.1369052, 2.29954689)]
COS = [root2 * v for v in (0.99940322, -4.89118661, 3.5838431)]


def far_values(turns, scale):
    part = turns - jnp.round(turns)
    z = part * part
    s = part * (((z * -0.55463616 + 2.54189901) * z + -5.16714279) * z + 3.14158202)
    c = ((z * -1.22212692 + 4.04128377) * z + -4.93393801) * z + 0.9999933
    s2 = s + s
    return (scale * (s2 * c)).astype(BF), (scale * (1.0 - s2 * s)).astype(BF)


def sin_cos(turns):
    part = turns - jnp.round(turns)
    quarter = jnp.round(4.0 * part)
    y = (part - 0.25 * quarter) * two_pi
    z = y * y
    s = y * (1.0 + z * (-1.0 / 6 + z * (1.0 / 120 + z * (-1.0 / 5040 + z * (1.0 / 362880)))))
    c = 1.0 + z * (-0.5 + z * (1.0 / 24 + z * (-1.0 / 720 + z * (1.0 / 40320))))
    odd = jnp.abs(quarter) == 1.0
    sin_v = jnp.where(odd, c, s)
    cos_v = jnp.where(odd, s, c)
    sin_v = jnp.where((quarter == -1.0) | (jnp.abs(quarter) == 2.0), -sin_v, sin_v)
    cos_v = jnp.where((quarter == 1.0) | (jnp.abs(quarter) == 2.0), -cos_v, cos_v)
    return sin_v, cos_v


ROWS = 512
COLS = 512
BLOCK = 256
MESH = pl.DeviceIdType.MESH


def turned(x):
    half = x.shape[1] // 2
    return jnp.concatenate([-x[:, half:], x[:, :half]], axis=1)


def incident(g, blades, harmonic):
    gt = g.T
    col = lambda i: gt[:, i : i + 1]
    source = lax.broadcasted_iota(jnp.int32, (1, NS), 1).astype(F32) * (1.0 / NS)
    sin_s, cos_s = sin_cos(source)
    dx = col(0) - cycle_radius * cos_s
    dy = col(1) - cycle_radius * sin_s
    dz = col(2) - cycle_height
    r_sq = dx * dx + dy * dy + dz * dz
    inv = lax.rsqrt(r_sq)
    sin_r, cos_r = sin_cos(r_sq * inv * kappa)
    g_re = cos_r * inv * (1.0 / four_pi)
    g_im = sin_r * inv * (1.0 / four_pi)
    f_re = (-g_re * inv - wavenumber * g_im) * inv
    f_im = (-g_im * inv + wavenumber * g_re) * inv
    along = (dx * col(3) + dy * col(4) + dz * col(5)) * (1.0 / wavenumber)
    h = jnp.concatenate([g_re - f_im * along, g_im + f_re * along], axis=1)
    modes = blades * harmonic
    at = lax.broadcasted_iota(jnp.int32, (NS, modes.shape[1]), 0)
    e_im, e_re = sin_cos(((at * modes) % NS).astype(F32) * (1.0 / NS))
    e = jnp.concatenate(
        [jnp.concatenate([e_re, e_im], axis=1), jnp.concatenate([-e_im, e_re], axis=1)], axis=0
    )
    return jnp.dot(h, e, precision=lax.Precision.HIGHEST, preferred_element_type=F32)


def correction(x, index, weight):
    count, n = index.shape
    both = jnp.concatenate([index.astype(F32), weight], axis=0).T
    lane = lax.broadcasted_iota(jnp.int32, (n, n), 1).astype(F32)
    w_re = jnp.zeros((n, n), F32)
    w_im = jnp.zeros((n, n), F32)
    for c in range(count):
        hit = lane == both[:, c : c + 1]
        w_re += jnp.where(hit, both[:, count + c : count + c + 1], 0.0)
        w_im += jnp.where(hit, both[:, 2 * count + c : 2 * count + c + 1], 0.0)
    x2 = jnp.concatenate([x, turned(x)], axis=0)
    total = jnp.zeros((n, x.shape[1]), F32)
    for part in pieces(jnp.concatenate([w_re, w_im], axis=1)):
        total += dot(part.astype(BF), x2)
    return total


def kernel(
    nrows, ncols, left_a, left_b, r0, r1, r2, r3, r4, t0, t1, t2, t3,
    krylov, geometry, corr_index, corr_weight, blades, harmonic, angles,
    out, far_out,
    cgeo, rgeo, x2, p0, p1, p2, p3, p4, p5, acc, acc2, acc3, base,
    stage, far_stage, part_in, far_in,
    send_sem, cgeo_sem, rgeo_sem, x_sem, far_sem, part_sem,
):
    rights = (r0, r1, r2, r3, r4)
    planes = ((p0, p1, p2), (p3, p4, p5))
    tiles = (t0, t1, t2, t3)
    accs = (acc, acc2, acc3)
    r = lax.axis_index("rows")
    c = lax.axis_index("cols")
    core = r % 2
    chip = r // 2
    chips = nrows // 2
    sibling = r + 1 - 2 * core
    n_cols = nrows * BLOCK
    n_rows = ncols * BLOCK
    n_obs = far_stage.shape[0]
    obs = n_obs // ncols
    steps = n_cols // COLS
    half = COLS // LANES
    panels = nrows * ncols * BLOCK
    sends = []
    first_forward = (nrows - 1) + 3 * (ncols - 1) + chips

    def send(src, dst, sem, row, col):
        copy = pltpu.make_async_remote_copy(
            src_ref=src, dst_ref=dst, send_sem=send_sem.at[len(sends)], recv_sem=sem,
            device_id=(row, col), device_id_type=MESH,
        )
        copy.start()
        sends.append(copy)

    def forward(k, at):
        return pltpu.make_async_remote_copy(
            src_ref=x2.at[at // 2, at % 2], dst_ref=x2.at[(chips + at) // 2, at % 2],
            send_sem=send_sem.at[first_forward + k - 1], recv_sem=x_sem.at[chips + at],
            device_id=(sibling, c), device_id_type=MESH,
        )

    def arrived(dst, sem):
        pltpu.make_async_remote_copy(
            src_ref=dst, dst_ref=dst, send_sem=send_sem.at[0], recv_sem=sem,
            device_id=(r, c), device_id_type=MESH,
        ).wait_recv()

    barrier = pltpu.get_barrier_semaphore()
    for k in range(1, nrows):
        pl.semaphore_signal(barrier, inc=1, device_id=((r + k) % nrows, c), device_id_type=MESH)
    for k in range(1, ncols):
        pl.semaphore_signal(barrier, inc=1, device_id=(r, (c + k) % ncols), device_id_type=MESH)

    ang = angles[:, pl.ds(pl.multiple_of(r * n_obs, n_obs), n_obs)] * (1.0 / two_pi)
    sin_t, cos_t = sin_cos(ang[0:1])
    sin_p, cos_p = sin_cos(ang[1:2])
    e = jnp.concatenate([sin_t * cos_p, sin_t * sin_p, cos_t, jnp.zeros((5, n_obs), F32)], axis=0)
    left_a[pl.ds(n_rows, n_obs), :] = left_stack(e).T.astype(BF)
    cgeo[chip] = geometry[...]
    rgeo[c] = geometry[...]
    x2[chip // 2, chip % 2] = krylov[...]

    x = krylov[...]
    index = corr_index[...] - (r * ncols + c) * BLOCK
    base[...] = -0.5 * x.astype(F32) - correction(x, index, corr_weight[...])
    own = jnp.concatenate([geometry[...], jnp.zeros((1, BLOCK), F32)], axis=0)
    base[...] += incident(own, blades[...], harmonic[...])

    pl.semaphore_wait(barrier, nrows + ncols - 2)
    for k in range(1, nrows):
        peer = (r + k) % nrows
        at = (r + peer) % 2 * chips + chip
        send(geometry, cgeo.at[at], cgeo_sem.at[at], peer, c)
    for k in range(1, ncols):
        send(geometry, rgeo.at[c], rgeo_sem.at[c], r, (c + k) % ncols)

    for k in range(1, nrows):
        at = (chip + k) % nrows
        arrived(cgeo.at[at], cgeo_sem.at[at])
    for k in range(1, ncols):
        at = (c + k) % ncols
        arrived(rgeo.at[at], rgeo_sem.at[at])
    send(krylov, x2.at[(chips + chip) // 2, chip % 2], x_sem.at[chips + chip], sibling, c)
    for k in range(1, chips):
        peer = (chip + k) % chips * 2 + core
        send(krylov, x2.at[chip // 2, chip % 2], x_sem.at[chip], peer, c)
    g = jnp.concatenate([cgeo[i] for i in range(nrows)], axis=1)
    g = jnp.concatenate([g, jnp.zeros((1, n_cols), F32)], axis=0)
    for ref, v in zip(rights, right_features(g)):
        ref[...] = v
    g = jnp.concatenate([rgeo[i] for i in range(ncols)], axis=1)
    g = jnp.concatenate([g, jnp.zeros((1, n_rows), F32)], axis=0)
    la, lb = left_features(g, 4.0 / panels)
    left_a[pl.ds(0, n_rows), :] = la.T.astype(BF)
    left_b[...] = lb.T.astype(BF)

    def make_geometry(first, step, far, into):
        cols = pl.ds(pl.multiple_of(step * COLS, COLS), COLS)
        rows = pl.ds(pl.multiple_of(first, ROWS), ROWS)
        la = left_a[rows, :]
        if far:
            into[0][...] = dot(la, rights[3][:, cols])
            into[1][...] = dot(la, rights[4][:, cols])
        else:
            into[0][...] = dot(la, rights[0][:, cols])
            into[1][...] = dot(la, rights[1][:, cols])
            into[2][...] = dot(left_b[rows, :], rights[2][:, cols])

    def make_values(step, far, frm, tile):
        if far:
            re, im = far_values(frm[0][...], frm[1][...])
        else:
            re, im = operator_tile(frm[0][...], frm[1][...], frm[2][...])
        for h in range(half):
            tile[step * 2 * half + h] = re[:, h * LANES : (h + 1) * LANES]
            tile[step * 2 * half + half + h] = im[:, h * LANES : (h + 1) * LANES]

    def product(step, tile, rows):
        lhs = jnp.concatenate([tile[step * 2 * half + h, rows, :] for h in range(2 * half)], axis=1)
        return dot(lhs, x2[step].reshape(2 * COLS, x2.shape[-1]))

    every = pl.ds(0, ROWS)
    pair = c // 2
    far_z, near_z = (1 - pair // 2) * 2, pair // 2 * 2
    where = [far_z + pair % 2, far_z + 1 - pair % 2, near_z + 1 - pair % 2, pair]
    blocks = len(where)
    seq = [(n_rows, True)] + [(w * ROWS, False) for w in where]
    multiplied = {3: (0, 1, 2), 4: (3,)}

    def prepare(step):
        for b in range(2):
            x2[step, 2 + b] = turned(x2[step, b])

    def run(ph, first_h, last_h):
        @pl.loop(first_h, last_h)
        def _(h):
            for par in range(2):
                step = 2 * h + par
                first, far = seq[ph]
                make_geometry(first, lax.rem(step + 1, steps), far, planes[1 - par])
                make_values(step, far, planes[par], tiles[ph % 4])
                for i, which in enumerate(multiplied.get(ph, ())):
                    accs[i][...] += product(step, tiles[which % 4], every)

    def pass_on():
        for k in range(1, chips):
            at = (chip + chips - k) % chips
            arrived(x2.at[at // 2, at % 2], x_sem.at[at])
            forward(k, at).start()
        for step in range(steps // 2):
            prepare(step)

    def take_passed():
        for k in range(chips, nrows):
            arrived(x2.at[k // 2, k % 2], x_sem.at[k])
        for step in range(steps // 2, steps):
            prepare(step)

    def send_parts(block):
        for b in range(2):
            owner = where[block] * 2 + b
            send(stage.at[owner], part_in.at[c], part_sem.at[c], r, owner)

    def keep_parts(block, total):
        for b in range(2):
            stage[where[block] * 2 + b] = total[pl.ds(b * BLOCK, BLOCK), :].astype(BF)

    for ph in range(len(seq)):
        first, far = seq[ph]
        make_geometry(first, 0, far, planes[0])
        for i in range(len(multiplied.get(ph, ()))):
            accs[i][...] = jnp.zeros_like(accs[i])
        if ph == 4:
            for k in range(1, ncols):
                owner = (c + k) % ncols
                rows = pl.ds(pl.multiple_of(owner * obs, obs), obs)
                send(far_stage.at[rows, :], far_in.at[c], far_sem.at[c], r, owner)
            send_parts(0)
            send_parts(1)
        if ph == 3:
            run(ph, 0, steps // 4)
            take_passed()
            run(ph, steps // 4, steps // 2)
            far_stage[...] = accs[0][...]
            keep_parts(0, accs[1])
            keep_parts(1, accs[2])
        else:
            run(ph, 0, steps // 2)
        if ph == 2:
            pass_on()
    keep_parts(2, accs[0])

    tile = tiles[(len(seq) - 1) % 4]
    same = lax.broadcasted_iota(jnp.int32, (BLOCK, LANES), 0)
    lane = lax.broadcasted_iota(jnp.int32, (BLOCK, LANES), 1)
    rows = pl.ds(pl.multiple_of(c % 2 * BLOCK, BLOCK), BLOCK)
    for h in range(BLOCK // LANES):
        for part in range(2):
            at = chip // 2 * 2 * half + part * half + chip % 2 * (BLOCK // LANES) + h
            v = tile[at, rows, :].astype(F32)
            tile[at, rows, :] = jnp.where(same == lane + h * LANES, 0.0, v).astype(BF)

    send_parts(2)
    partner = c + 1 - 2 * (c % 2)
    mine = acc.at[pl.ds(0, BLOCK), :]
    theirs = acc.at[pl.ds(BLOCK, BLOCK), :]
    other_rows = pl.ds(pl.multiple_of((1 - c % 2) * BLOCK, BLOCK), BLOCK)
    theirs[...] = product(0, tile, other_rows)

    @pl.loop(1, steps)
    def _(step):
        theirs[...] += product(step, tile, other_rows)

    stage[partner] = theirs[...].astype(BF)
    mine[...] = product(0, tile, rows)
    send(stage.at[partner], part_in.at[c], part_sem.at[c], r, partner)

    @pl.loop(1, steps)
    def _(step):
        mine[...] += product(step, tile, rows)

    total = far_stage[pl.ds(pl.multiple_of(c * obs, obs), obs), :]
    for k in range(1, ncols):
        at = (c + ncols - k) % ncols
        arrived(far_in.at[at], far_sem.at[at])
        total += far_in[at]
    far_out[...] = total
    total = base[...] - mine[...]
    for k in range(1, ncols):
        at = (c + ncols - k) % ncols
        arrived(part_in.at[at], part_sem.at[at])
        total -= part_in[at].astype(F32)
    out[...] = total
    for copy in sends:
        copy.wait_send()
    for k in range(1, chips):
        forward(k, (chip + chips - k) % chips).wait_send()


def local(krylov, geometry, corr_index, corr_weight, blades, harmonic, observer_angles):
    nrows = lax.axis_size("rows")
    ncols = lax.axis_size("cols")
    width = krylov.shape[1]
    n_cols, n_rows = nrows * BLOCK, ncols * BLOCK
    n_obs = observer_angles.shape[1] // nrows
    n_sends = (nrows - 1) + 4 * (ncols - 1) + nrows
    scoped = (
        [pltpu.VMEM((n_rows + n_obs, 48), BF), pltpu.VMEM((n_rows, 48), BF)]
        + [pltpu.VMEM((48, n_cols), BF)] * 5
        + [pltpu.VMEM((2 * n_cols // LANES, ROWS, LANES), BF)] * 4
    )

    def body(*refs):
        pl.run_scoped(lambda *own: kernel(nrows, ncols, *own, *refs), *scoped)

    vm = pl.BlockSpec(memory_space=pltpu.VMEM)
    dma = pltpu.SemaphoreType.DMA
    return pl.pallas_call(
        body,
        out_shape=(
            jax.ShapeDtypeStruct((BLOCK, width), F32),
            jax.ShapeDtypeStruct((n_obs // ncols, width), F32),
        ),
        in_specs=[vm] * 7,
        out_specs=(vm, vm),
        scratch_shapes=[
            pltpu.VMEM((nrows, 7, BLOCK), F32),
            pltpu.VMEM((ncols, 7, BLOCK), F32),
        ]
        + [pltpu.VMEM((n_cols // COLS, 4, BLOCK, width), BF)]
        + [pltpu.VMEM((ROWS, COLS), F32)] * 6
        + [
            pltpu.VMEM((ROWS, width), F32),
            pltpu.VMEM((ROWS, width), F32),
            pltpu.VMEM((ROWS, width), F32),
            pltpu.VMEM((BLOCK, width), F32),
            pltpu.VMEM((ncols, BLOCK, width), BF),
            pltpu.VMEM((n_obs, width), F32),
            pltpu.VMEM((ncols, BLOCK, width), BF),
            pltpu.VMEM((ncols, n_obs // ncols, width), F32),
            dma((n_sends,)),
            dma((nrows,)),
            dma((ncols,)),
            dma((nrows,)),
            dma((ncols,)),
            dma((ncols,)),
        ],
        compiler_params=pltpu.CompilerParams(
            collective_id=0, has_side_effects=True, vmem_limit_bytes=60 << 20
        ),
        name="burton_miller",
    )(krylov, geometry, corr_index, corr_weight, blades[None], harmonic[None], observer_angles)


def solution(mesh):
    placed = (
        P(("rows", "cols"), None),
        P(None, ("rows", "cols")),
        P(None, ("rows", "cols")),
        P(None, ("rows", "cols")),
        P(),
        P(),
        P(),
    )
    return jax.shard_map(
        local,
        mesh=mesh,
        in_specs=placed,
        out_specs=(P(("rows", "cols"), None), P(("rows", "cols"), None)),
        check_vma=False,
    )
```

```python
import functools
import math

import jax
import jax.numpy as jnp
from jax import lax
from jax.experimental import pallas as pl
from jax.experimental.pallas import tpu as pltpu
from jax.sharding import PartitionSpec as P

BF = jnp.bfloat16
F32 = jnp.float32
NS = 64
LANES = 128

wavenumber = 20.0
cycle_radius = 0.7
cycle_height = 1.0
four_pi = 4.0 * math.pi
two_pi = 2.0 * math.pi
kappa = wavenumber / two_pi

dot = functools.partial(jnp.dot, preferred_element_type=F32)


def pieces(x):
    first = x.astype(BF).astype(F32)
    rest = x - first
    second = rest.astype(BF).astype(F32)
    return first, second, (rest - second).astype(BF).astype(F32)


def left_stack(x):
    a, b, c = pieces(x)
    return jnp.concatenate([a, a, b, a, c, b], axis=0)


def right_stack(x):
    a, b, c = pieces(x)
    return jnp.concatenate([a, b, a, c, a, b], axis=0).astype(BF)


def panel_rows(g):
    row = lax.broadcasted_iota(jnp.int32, g.shape, 0)
    center = row < 3
    normal = pltpu.roll(g, 5, 0)
    c_sq = jnp.sum(jnp.where(center, g * g, 0.0), axis=0, keepdims=True)
    n_c = jnp.sum(jnp.where(center, g * normal, 0.0), axis=0, keepdims=True)
    return row, center, normal, c_sq, n_c, g[6:7]


def left_features(g, soft_sq):
    row, center, normal, c_sq, n_c, _ = panel_rows(g)
    size = (kappa * kappa) * (c_sq + soft_sq)
    one = jnp.where(row == 3, 1.0, jnp.where(row == 4, size, 0.0))
    two = jnp.where(row == 3, n_c, 0.0)
    return (
        left_stack(jnp.where(center, g, one)),
        left_stack(jnp.where(center, normal, two)),
    )


def right_features(g):
    row, center, normal, c_sq, n_c, area = panel_rows(g)
    scale = area * (kappa * kappa / four_pi)
    k_sq = kappa * kappa
    r_sq = jnp.where(
        center, -2.0 * k_sq * g, jnp.where(row == 3, k_sq * c_sq, jnp.where(row == 4, 1.0, 0.0))
    )
    along_col = jnp.where(
        center, -wavenumber * scale * normal, jnp.where(row == 3, wavenumber * scale * n_c, 0.0)
    )
    along_row = jnp.where(center, scale * g, jnp.where(row == 3, -scale, 0.0))
    far_turns = jnp.where(center, kappa * g, 0.0)
    far_scale = jnp.where(center, -wavenumber * area * normal, 0.0)
    return [right_stack(v) for v in (r_sq, along_col, along_row, far_turns, far_scale)]


def operator_tile(r_sq, along_col, along_row):
    inv = lax.rsqrt(r_sq)
    turns = r_sq * inv
    part = (turns - jnp.round(turns)).astype(BF)
    u = inv.astype(BF)
    a = along_col.astype(BF)
    b = along_row.astype(BF)

    def const(v):
        return jnp.asarray(v, BF)

    z = part * part
    sin_poly = (z * const(SIN[2]) + const(SIN[1])) * z + const(SIN[0])
    cos_poly = (z * const(COS[2]) + const(COS[1])) * z + const(COS[0])
    s = (part * u) * sin_poly
    c = u * cos_poly
    re = u * u - s * s
    im = s * c
    w = u * const(1.0 / two_pi)
    p = b - w * a
    q = a + w * b
    return re * p - im * q, re * q + im * p


root2 = math.sqrt(2.0)
SIN = [root2 * v for v in (3.14064003, -5.1369052, 2.29954689)]
COS = [root2 * v for v in (0.99940322, -4.89118661, 3.5838431)]


def far_values(turns, scale):
    part = turns - jnp.round(turns)
    z = part * part
    s = part * (((z * -0.55463616 + 2.54189901) * z + -5.16714279) * z + 3.14158202)
    c = ((z * -1.22212692 + 4.04128377) * z + -4.93393801) * z + 0.9999933
    s2 = s + s
    return (scale * (s2 * c)).astype(BF), (scale * (1.0 - s2 * s)).astype(BF)


def sin_cos(turns):
    part = turns - jnp.round(turns)
    quarter = jnp.round(4.0 * part)
    y = (part - 0.25 * quarter) * two_pi
    z = y * y
    s = y * (1.0 + z * (-1.0 / 6 + z * (1.0 / 120 + z * (-1.0 / 5040 + z * (1.0 / 362880)))))
    c = 1.0 + z * (-0.5 + z * (1.0 / 24 + z * (-1.0 / 720 + z * (1.0 / 40320))))
    odd = jnp.abs(quarter) == 1.0
    sin_v = jnp.where(odd, c, s)
    cos_v = jnp.where(odd, s, c)
    sin_v = jnp.where((quarter == -1.0) | (jnp.abs(quarter) == 2.0), -sin_v, sin_v)
    cos_v = jnp.where((quarter == 1.0) | (jnp.abs(quarter) == 2.0), -cos_v, cos_v)
    return sin_v, cos_v


ROWS = 512
COLS = 512
BLOCK = 256
MESH = pl.DeviceIdType.MESH


def turned(x):
    half = x.shape[1] // 2
    return jnp.concatenate([-x[:, half:], x[:, :half]], axis=1)


def incident(g, blades, harmonic):
    gt = g.T
    col = lambda i: gt[:, i : i + 1]
    source = lax.broadcasted_iota(jnp.int32, (1, NS), 1).astype(F32) * (1.0 / NS)
    sin_s, cos_s = sin_cos(source)
    dx = col(0) - cycle_radius * cos_s
    dy = col(1) - cycle_radius * sin_s
    dz = col(2) - cycle_height
    r_sq = dx * dx + dy * dy + dz * dz
    inv = lax.rsqrt(r_sq)
    sin_r, cos_r = sin_cos(r_sq * inv * kappa)
    g_re = cos_r * inv * (1.0 / four_pi)
    g_im = sin_r * inv * (1.0 / four_pi)
    f_re = (-g_re * inv - wavenumber * g_im) * inv
    f_im = (-g_im * inv + wavenumber * g_re) * inv
    along = (dx * col(3) + dy * col(4) + dz * col(5)) * (1.0 / wavenumber)
    h = jnp.concatenate([g_re - f_im * along, g_im + f_re * along], axis=1)
    modes = blades * harmonic
    at = lax.broadcasted_iota(jnp.int32, (NS, modes.shape[1]), 0)
    e_im, e_re = sin_cos(((at * modes) % NS).astype(F32) * (1.0 / NS))
    e = jnp.concatenate(
        [jnp.concatenate([e_re, e_im], axis=1), jnp.concatenate([-e_im, e_re], axis=1)], axis=0
    )
    return jnp.dot(h, e, precision=lax.Precision.HIGHEST, preferred_element_type=F32)


def correction(x, index, weight):
    count, n = index.shape
    both = jnp.concatenate([index.astype(F32), weight], axis=0).T
    lane = lax.broadcasted_iota(jnp.int32, (n, n), 1).astype(F32)
    w_re = jnp.zeros((n, n), F32)
    w_im = jnp.zeros((n, n), F32)
    for c in range(count):
        hit = lane == both[:, c : c + 1]
        w_re += jnp.where(hit, both[:, count + c : count + c + 1], 0.0)
        w_im += jnp.where(hit, both[:, 2 * count + c : 2 * count + c + 1], 0.0)
    x2 = jnp.concatenate([x, turned(x)], axis=0)
    total = jnp.zeros((n, x.shape[1]), F32)
    for part in pieces(jnp.concatenate([w_re, w_im], axis=1)):
        total += dot(part.astype(BF), x2)
    return total


def kernel(
    nrows, ncols, left_a, left_b, r0, r1, r2, r3, r4, t0, t1, t2, t3,
    krylov, geometry, corr_index, corr_weight, blades, harmonic, angles,
    out, far_out,
    cgeo, rgeo, x2, p0, p1, p2, p3, p4, p5, acc, acc2, acc3, base,
    stage, far_stage, part_in, far_in,
    send_sem, cgeo_sem, rgeo_sem, x_sem, far_sem, part_sem,
):
    rights = (r0, r1, r2, r3, r4)
    planes = ((p0, p1, p2), (p3, p4, p5))
    tiles = (t0, t1, t2, t3)
    accs = (acc, acc2, acc3)
    r = lax.axis_index("rows")
    c = lax.axis_index("cols")
    core = r % 2
    chip = r // 2
    chips = nrows // 2
    sibling = r + 1 - 2 * core
    n_cols = nrows * BLOCK
    n_rows = ncols * BLOCK
    n_obs = far_stage.shape[0]
    obs = n_obs // ncols
    steps = n_cols // COLS
    half = COLS // LANES
    panels = nrows * ncols * BLOCK
    sends = []
    first_forward = (nrows - 1) + 3 * (ncols - 1) + chips

    def send(src, dst, sem, row, col):
        copy = pltpu.make_async_remote_copy(
            src_ref=src, dst_ref=dst, send_sem=send_sem.at[len(sends)], recv_sem=sem,
            device_id=(row, col), device_id_type=MESH,
        )
        copy.start()
        sends.append(copy)

    def forward(k, at):
        return pltpu.make_async_remote_copy(
            src_ref=x2.at[at // 2, at % 2], dst_ref=x2.at[(chips + at) // 2, at % 2],
            send_sem=send_sem.at[first_forward + k - 1], recv_sem=x_sem.at[chips + at],
            device_id=(sibling, c), device_id_type=MESH,
        )

    def arrived(dst, sem):
        pltpu.make_async_remote_copy(
            src_ref=dst, dst_ref=dst, send_sem=send_sem.at[0], recv_sem=sem,
            device_id=(r, c), device_id_type=MESH,
        ).wait_recv()

    barrier = pltpu.get_barrier_semaphore()
    for k in range(1, nrows):
        pl.semaphore_signal(barrier, inc=1, device_id=((r + k) % nrows, c), device_id_type=MESH)
    for k in range(1, ncols):
        pl.semaphore_signal(barrier, inc=1, device_id=(r, (c + k) % ncols), device_id_type=MESH)

    ang = angles[:, pl.ds(pl.multiple_of(r * n_obs, n_obs), n_obs)] * (1.0 / two_pi)
    sin_t, cos_t = sin_cos(ang[0:1])
    sin_p, cos_p = sin_cos(ang[1:2])
    e = jnp.concatenate([sin_t * cos_p, sin_t * sin_p, cos_t, jnp.zeros((5, n_obs), F32)], axis=0)
    left_a[pl.ds(n_rows, n_obs), :] = left_stack(e).T.astype(BF)
    cgeo[chip] = geometry[...]
    rgeo[c] = geometry[...]
    x2[chip // 2, chip % 2] = krylov[...]

    x = krylov[...]
    index = corr_index[...] - (r * ncols + c) * BLOCK
    base[...] = -0.5 * x.astype(F32) - correction(x, index, corr_weight[...])
    own = jnp.concatenate([geometry[...], jnp.zeros((1, BLOCK), F32)], axis=0)
    base[...] += incident(own, blades[...], harmonic[...])

    pl.semaphore_wait(barrier, nrows + ncols - 2)
    for k in range(1, nrows):
        peer = (r + k) % nrows
        at = (r + peer) % 2 * chips + chip
        send(geometry, cgeo.at[at], cgeo_sem.at[at], peer, c)
    for k in range(1, ncols):
        send(geometry, rgeo.at[c], rgeo_sem.at[c], r, (c + k) % ncols)

    for k in range(1, nrows):
        at = (chip + k) % nrows
        arrived(cgeo.at[at], cgeo_sem.at[at])
    for k in range(1, ncols):
        at = (c + k) % ncols
        arrived(rgeo.at[at], rgeo_sem.at[at])
    send(krylov, x2.at[(chips + chip) // 2, chip % 2], x_sem.at[chips + chip], sibling, c)
    for k in range(1, chips):
        peer = (chip + k) % chips * 2 + core
        send(krylov, x2.at[chip // 2, chip % 2], x_sem.at[chip], peer, c)
    g = jnp.concatenate([cgeo[i] for i in range(nrows)], axis=1)
    g = jnp.concatenate([g, jnp.zeros((1, n_cols), F32)], axis=0)
    for ref, v in zip(rights, right_features(g)):
        ref[...] = v
    g = jnp.concatenate([rgeo[i] for i in range(ncols)], axis=1)
    g = jnp.concatenate([g, jnp.zeros((1, n_rows), F32)], axis=0)
    la, lb = left_features(g, 4.0 / panels)
    left_a[pl.ds(0, n_rows), :] = la.T.astype(BF)
    left_b[...] = lb.T.astype(BF)

    def make_geometry(panel, step, into):
        first, far, count = panel
        cols = pl.ds(pl.multiple_of(step * COLS, COLS), COLS)
        rows = pl.ds(pl.multiple_of(first, BLOCK), count)
        top = pl.ds(0, count)
        la = left_a[rows, :]
        if far:
            into[0][top, :] = dot(la, rights[3][:, cols])
            into[1][top, :] = dot(la, rights[4][:, cols])
        else:
            into[0][top, :] = dot(la, rights[0][:, cols])
            into[1][top, :] = dot(la, rights[1][:, cols])
            into[2][top, :] = dot(left_b[rows, :], rights[2][:, cols])

    def make_values(panel, step, frm, tile):
        _, far, count = panel
        top = pl.ds(0, count)
        if far:
            re, im = far_values(frm[0][top, :], frm[1][top, :])
        else:
            re, im = operator_tile(frm[0][top, :], frm[1][top, :], frm[2][top, :])
        for h in range(half):
            tile[step * 2 * half + h, top, :] = re[:, h * LANES : (h + 1) * LANES]
            tile[step * 2 * half + half + h, top, :] = im[:, h * LANES : (h + 1) * LANES]

    def product(step, tile, rows):
        lhs = jnp.concatenate([tile[step * 2 * half + h, rows, :] for h in range(2 * half)], axis=1)
        return dot(lhs, x2[step].reshape(2 * COLS, x2.shape[-1]))

    every = pl.ds(0, ROWS)
    pair = c // 2
    far_z, near_z = (1 - pair // 2) * 2, pair // 2 * 2
    where = [far_z + pair % 2, far_z + 1 - pair % 2, near_z + 1 - pair % 2, pair]
    partner = c + 1 - 2 * (c % 2)
    seq = [(n_rows, True, ROWS)] + [(w * ROWS, False, ROWS) for w in where[:-1]]
    seq += [(partner * BLOCK, False, BLOCK), (c * BLOCK, False, BLOCK)]

    def prepare(step):
        for b in range(2):
            x2[step, 2 + b] = turned(x2[step, b])

    def two_steps(ph, h, products, between=None):
        for par in range(2):
            step = 2 * h + par
            make_geometry(seq[ph], lax.rem(step + 1, steps), planes[1 - par])
            if par == 0 and between is not None:
                between()
            make_values(seq[ph], step, planes[par], tiles[ph % 4])
            for which, at, total, rows in products(step, par):
                total[rows, :] += product(at, tiles[which % 4], rows)

    def run(ph, products):
        @pl.loop(0, steps // 2)
        def _(h):
            two_steps(ph, h, products)

    def pass_on():
        for k in range(1, chips):
            at = (chip + chips - k) % chips
            arrived(x2.at[at // 2, at % 2], x_sem.at[at])
            forward(k, at).start()
        for step in range(steps // 2):
            prepare(step)

    def take_passed():
        for k in range(chips, nrows):
            arrived(x2.at[k // 2, k % 2], x_sem.at[k])
        for step in range(steps // 2, steps):
            prepare(step)

    def send_parts(block):
        for b in range(2):
            owner = where[block] * 2 + b
            send(stage.at[owner], part_in.at[c], part_sem.at[c], r, owner)

    def keep_parts(block, total):
        for b in range(2):
            stage[where[block] * 2 + b] = total[pl.ds(b * BLOCK, BLOCK), :].astype(BF)

    def send_far():
        for k in range(1, ncols):
            owner = (c + k) % ncols
            rows = pl.ds(pl.multiple_of(owner * obs, obs), obs)
            send(far_stage.at[rows, :], far_in.at[c], far_sem.at[c], r, owner)

    def catch_up(first):
        listed = [(w, first + i, accs[w], every) for w in range(3) for i in range(steps // 2)]
        each = len(listed) // (steps // 2)
        return lambda h, par: listed[(2 * h + par) * each : (2 * h + par + 1) * each]

    top = pl.ds(0, BLOCK)
    for ph in range(len(seq)):
        make_geometry(seq[ph], 0, planes[0])
        if ph < 3:
            run(ph, lambda step, par: ())
            if ph == 2:
                pass_on()
        elif ph == 3:
            for total in accs:
                total[...] = jnp.zeros_like(total)
            for part in range(2):
                todo = catch_up(part * (steps // 2))
                for h in range(steps // 4):
                    last = part == 1 and h == 1
                    if last:
                        far_stage[...] = accs[0][...]
                    two_steps(
                        ph, part * (steps // 4) + h, lambda step, par, h=h, todo=todo: todo(h, par), send_far if last else None
                    )
                if part == 0:
                    take_passed()
            keep_parts(0, accs[1])
            keep_parts(1, accs[2])
        elif ph == 4:
            accs[0][...] = jnp.zeros_like(accs[0])
            send_parts(0)
            send_parts(1)
            run(ph, lambda step, par: ((3, step, accs[0], every),))
            keep_parts(2, accs[0])
        else:
            accs[1][top, :] = jnp.zeros((BLOCK, acc.shape[1]), F32)
            send_parts(2)
            run(ph, lambda step, par: ((4, step, accs[1], top),))
            stage[partner] = accs[1][top, :].astype(BF)

    tile = tiles[(len(seq) - 1) % 4]
    same = lax.broadcasted_iota(jnp.int32, (BLOCK, LANES), 0)
    lane = lax.broadcasted_iota(jnp.int32, (BLOCK, LANES), 1)
    for h in range(BLOCK // LANES):
        for part in range(2):
            at = chip // 2 * 2 * half + part * half + chip % 2 * (BLOCK // LANES) + h
            v = tile[at, top, :].astype(F32)
            tile[at, top, :] = jnp.where(same == lane + h * LANES, 0.0, v).astype(BF)

    mine = acc.at[top, :]
    mine[...] = product(0, tile, top)
    send(stage.at[partner], part_in.at[c], part_sem.at[c], r, partner)

    @pl.loop(1, steps)
    def _(step):
        mine[...] += product(step, tile, top)

    total = far_stage[pl.ds(pl.multiple_of(c * obs, obs), obs), :]
    for k in range(1, ncols):
        at = (c + ncols - k) % ncols
        arrived(far_in.at[at], far_sem.at[at])
        total += far_in[at]
    far_out[...] = total
    total = base[...] - mine[...]
    for k in range(1, ncols):
        at = (c + ncols - k) % ncols
        arrived(part_in.at[at], part_sem.at[at])
        total -= part_in[at].astype(F32)
    out[...] = total
    for copy in sends:
        copy.wait_send()
    for k in range(1, chips):
        forward(k, (chip + chips - k) % chips).wait_send()


def local(krylov, geometry, corr_index, corr_weight, blades, harmonic, observer_angles):
    nrows = lax.axis_size("rows")
    ncols = lax.axis_size("cols")
    width = krylov.shape[1]
    n_cols, n_rows = nrows * BLOCK, ncols * BLOCK
    n_obs = observer_angles.shape[1] // nrows
    n_sends = (nrows - 1) + 4 * (ncols - 1) + nrows
    scoped = (
        [pltpu.VMEM((n_rows + n_obs, 48), BF), pltpu.VMEM((n_rows, 48), BF)]
        + [pltpu.VMEM((48, n_cols), BF)] * 5
        + [pltpu.VMEM((2 * n_cols // LANES, ROWS, LANES), BF)] * 4
    )

    def body(*refs):
        pl.run_scoped(lambda *own: kernel(nrows, ncols, *own, *refs), *scoped)

    vm = pl.BlockSpec(memory_space=pltpu.VMEM)
    dma = pltpu.SemaphoreType.DMA
    return pl.pallas_call(
        body,
        out_shape=(
            jax.ShapeDtypeStruct((BLOCK, width), F32),
            jax.ShapeDtypeStruct((n_obs // ncols, width), F32),
        ),
        in_specs=[vm] * 7,
        out_specs=(vm, vm),
        scratch_shapes=[
            pltpu.VMEM((nrows, 7, BLOCK), F32),
            pltpu.VMEM((ncols, 7, BLOCK), F32),
        ]
        + [pltpu.VMEM((n_cols // COLS, 4, BLOCK, width), BF)]
        + [pltpu.VMEM((ROWS, COLS), F32)] * 6
        + [
            pltpu.VMEM((ROWS, width), F32),
            pltpu.VMEM((ROWS, width), F32),
            pltpu.VMEM((ROWS, width), F32),
            pltpu.VMEM((BLOCK, width), F32),
            pltpu.VMEM((ncols, BLOCK, width), BF),
            pltpu.VMEM((n_obs, width), F32),
            pltpu.VMEM((ncols, BLOCK, width), BF),
            pltpu.VMEM((ncols, n_obs // ncols, width), F32),
            dma((n_sends,)),
            dma((nrows,)),
            dma((ncols,)),
            dma((nrows,)),
            dma((ncols,)),
            dma((ncols,)),
        ],
        compiler_params=pltpu.CompilerParams(
            collective_id=0, has_side_effects=True, vmem_limit_bytes=60 << 20
        ),
        name="burton_miller",
    )(krylov, geometry, corr_index, corr_weight, blades[None], harmonic[None], observer_angles)


def solution(mesh):
    placed = (
        P(("rows", "cols"), None),
        P(None, ("rows", "cols")),
        P(None, ("rows", "cols")),
        P(None, ("rows", "cols")),
        P(),
        P(),
        P(),
    )
    return jax.shard_map(
        local,
        mesh=mesh,
        in_specs=placed,
        out_specs=(P(("rows", "cols"), None), P(("rows", "cols"), None)),
        check_vma=False,
    )
```

```python
import functools
import math

import jax
import jax.numpy as jnp
from jax import lax
from jax.experimental import pallas as pl
from jax.experimental.pallas import tpu as pltpu
from jax.sharding import PartitionSpec as P

BF = jnp.bfloat16
F32 = jnp.float32
NS = 64
LANES = 128

wavenumber = 20.0
cycle_radius = 0.7
cycle_height = 1.0
four_pi = 4.0 * math.pi
two_pi = 2.0 * math.pi
kappa = wavenumber / two_pi

dot = functools.partial(jnp.dot, preferred_element_type=F32)


def pieces(x):
    first = x.astype(BF).astype(F32)
    rest = x - first
    second = rest.astype(BF).astype(F32)
    return first, second, (rest - second).astype(BF).astype(F32)


def left_stack(x):
    a, b, c = pieces(x)
    return jnp.concatenate([a, a, b, a, c, b], axis=0)


def right_stack(x):
    a, b, c = pieces(x)
    return jnp.concatenate([a, b, a, c, a, b], axis=0).astype(BF)


def panel_rows(g):
    row = lax.broadcasted_iota(jnp.int32, g.shape, 0)
    center = row < 3
    normal = pltpu.roll(g, 5, 0)
    c_sq = jnp.sum(jnp.where(center, g * g, 0.0), axis=0, keepdims=True)
    n_c = jnp.sum(jnp.where(center, g * normal, 0.0), axis=0, keepdims=True)
    return row, center, normal, c_sq, n_c, g[6:7]


def left_features(g, soft_sq):
    row, center, normal, c_sq, n_c, _ = panel_rows(g)
    size = (kappa * kappa) * (c_sq + soft_sq)
    one = jnp.where(row == 3, 1.0, jnp.where(row == 4, size, 0.0))
    two = jnp.where(row == 3, n_c, 0.0)
    return (
        left_stack(jnp.where(center, g, one)),
        left_stack(jnp.where(center, normal, two)),
    )


def right_features(g):
    row, center, normal, c_sq, n_c, area = panel_rows(g)
    scale = area * (kappa * kappa / four_pi)
    k_sq = kappa * kappa
    r_sq = jnp.where(
        center, -2.0 * k_sq * g, jnp.where(row == 3, k_sq * c_sq, jnp.where(row == 4, 1.0, 0.0))
    )
    along_col = jnp.where(
        center, -wavenumber * scale * normal, jnp.where(row == 3, wavenumber * scale * n_c, 0.0)
    )
    along_row = jnp.where(center, scale * g, jnp.where(row == 3, -scale, 0.0))
    far_turns = jnp.where(center, kappa * g, 0.0)
    far_scale = jnp.where(center, -wavenumber * area * normal, 0.0)
    return [right_stack(v) for v in (r_sq, along_col, along_row, far_turns, far_scale)]


def operator_tile(r_sq, along_col, along_row):
    inv = lax.rsqrt(r_sq)
    turns = r_sq * inv
    part = (turns - jnp.round(turns)).astype(BF)
    u = inv.astype(BF)
    a = along_col.astype(BF)
    b = along_row.astype(BF)

    def const(v):
        return jnp.asarray(v, BF)

    z = part * part
    sin_poly = (z * const(SIN[2]) + const(SIN[1])) * z + const(SIN[0])
    cos_poly = (z * const(COS[2]) + const(COS[1])) * z + const(COS[0])
    s = (part * u) * sin_poly
    c = u * cos_poly
    re = u * u - s * s
    im = s * c
    w = u * const(1.0 / two_pi)
    p = b - w * a
    q = a + w * b
    return re * p - im * q, re * q + im * p


root2 = math.sqrt(2.0)
SIN = [root2 * v for v in (3.14064003, -5.1369052, 2.29954689)]
COS = [root2 * v for v in (0.99940322, -4.89118661, 3.5838431)]


def far_values(turns, scale):
    part = turns - jnp.round(turns)
    z = part * part
    s = part * (((z * -0.55463616 + 2.54189901) * z + -5.16714279) * z + 3.14158202)
    c = ((z * -1.22212692 + 4.04128377) * z + -4.93393801) * z + 0.9999933
    s2 = s + s
    return (scale * (s2 * c)).astype(BF), (scale * (1.0 - s2 * s)).astype(BF)


def sin_cos(turns):
    part = turns - jnp.round(turns)
    quarter = jnp.round(4.0 * part)
    y = (part - 0.25 * quarter) * two_pi
    z = y * y
    s = y * (1.0 + z * (-1.0 / 6 + z * (1.0 / 120 + z * (-1.0 / 5040 + z * (1.0 / 362880)))))
    c = 1.0 + z * (-0.5 + z * (1.0 / 24 + z * (-1.0 / 720 + z * (1.0 / 40320))))
    odd = jnp.abs(quarter) == 1.0
    sin_v = jnp.where(odd, c, s)
    cos_v = jnp.where(odd, s, c)
    sin_v = jnp.where((quarter == -1.0) | (jnp.abs(quarter) == 2.0), -sin_v, sin_v)
    cos_v = jnp.where((quarter == 1.0) | (jnp.abs(quarter) == 2.0), -cos_v, cos_v)
    return sin_v, cos_v


ROWS = 512
COLS = 512
BLOCK = 256
MESH = pl.DeviceIdType.MESH


def turned(x):
    half = x.shape[1] // 2
    return jnp.concatenate([-x[:, half:], x[:, :half]], axis=1)


def incident(g, blades, harmonic):
    gt = g.T
    col = lambda i: gt[:, i : i + 1]
    source = lax.broadcasted_iota(jnp.int32, (1, NS), 1).astype(F32) * (1.0 / NS)
    sin_s, cos_s = sin_cos(source)
    dx = col(0) - cycle_radius * cos_s
    dy = col(1) - cycle_radius * sin_s
    dz = col(2) - cycle_height
    r_sq = dx * dx + dy * dy + dz * dz
    inv = lax.rsqrt(r_sq)
    sin_r, cos_r = sin_cos(r_sq * inv * kappa)
    g_re = cos_r * inv * (1.0 / four_pi)
    g_im = sin_r * inv * (1.0 / four_pi)
    f_re = (-g_re * inv - wavenumber * g_im) * inv
    f_im = (-g_im * inv + wavenumber * g_re) * inv
    along = (dx * col(3) + dy * col(4) + dz * col(5)) * (1.0 / wavenumber)
    h = jnp.concatenate([g_re - f_im * along, g_im + f_re * along], axis=1)
    modes = blades * harmonic
    at = lax.broadcasted_iota(jnp.int32, (NS, modes.shape[1]), 0)
    e_im, e_re = sin_cos(((at * modes) % NS).astype(F32) * (1.0 / NS))
    e = jnp.concatenate(
        [jnp.concatenate([e_re, e_im], axis=1), jnp.concatenate([-e_im, e_re], axis=1)], axis=0
    )
    return jnp.dot(h, e, precision=lax.Precision.HIGHEST, preferred_element_type=F32)


def correction(x, index, weight):
    count, n = index.shape
    both = jnp.concatenate([index.astype(F32), weight], axis=0).T
    lane = lax.broadcasted_iota(jnp.int32, (n, n), 1).astype(F32)
    w_re = jnp.zeros((n, n), F32)
    w_im = jnp.zeros((n, n), F32)
    for c in range(count):
        hit = lane == both[:, c : c + 1]
        w_re += jnp.where(hit, both[:, count + c : count + c + 1], 0.0)
        w_im += jnp.where(hit, both[:, 2 * count + c : 2 * count + c + 1], 0.0)
    x2 = jnp.concatenate([x, turned(x)], axis=0)
    total = jnp.zeros((n, x.shape[1]), F32)
    for part in pieces(jnp.concatenate([w_re, w_im], axis=1)):
        total += dot(part.astype(BF), x2)
    return total


def kernel(
    nrows, ncols, left_a, left_b, r0, r1, r2, r3, r4, t0, t1, t2, t3,
    krylov, geometry, corr_index, corr_weight, blades, harmonic, angles,
    out, far_out,
    cgeo, rgeo, x2, p0, p1, p2, p3, p4, p5, acc, acc2, acc3, base,
    stage, far_stage, part_in, far_in,
    send_sem, cgeo_sem, rgeo_sem, x_sem, far_sem, part_sem,
):
    rights = (r0, r1, r2, r3, r4)
    planes = ((p0, p1, p2), (p3, p4, p5))
    tiles = (t0, t1, t2, t3)
    accs = (acc, acc2, acc3)
    r = lax.axis_index("rows")
    c = lax.axis_index("cols")
    core = r % 2
    chip = r // 2
    chips = nrows // 2
    sibling = r + 1 - 2 * core
    n_cols = nrows * BLOCK
    n_rows = ncols * BLOCK
    n_obs = far_stage.shape[0]
    obs = n_obs // ncols
    steps = n_cols // COLS
    half = COLS // LANES
    panels = nrows * ncols * BLOCK
    sends = []
    first_forward = (nrows - 1) + 3 * (ncols - 1) + chips

    def send(src, dst, sem, row, col):
        copy = pltpu.make_async_remote_copy(
            src_ref=src, dst_ref=dst, send_sem=send_sem.at[len(sends)], recv_sem=sem,
            device_id=(row, col), device_id_type=MESH,
        )
        copy.start()
        sends.append(copy)

    def forward(k, at):
        return pltpu.make_async_remote_copy(
            src_ref=x2.at[at // 2, at % 2], dst_ref=x2.at[(chips + at) // 2, at % 2],
            send_sem=send_sem.at[first_forward + k - 1], recv_sem=x_sem.at[chips + at],
            device_id=(sibling, c), device_id_type=MESH,
        )

    def arrived(dst, sem):
        pltpu.make_async_remote_copy(
            src_ref=dst, dst_ref=dst, send_sem=send_sem.at[0], recv_sem=sem,
            device_id=(r, c), device_id_type=MESH,
        ).wait_recv()

    barrier = pltpu.get_barrier_semaphore()
    for k in range(1, nrows):
        pl.semaphore_signal(barrier, inc=1, device_id=((r + k) % nrows, c), device_id_type=MESH)
    for k in range(1, ncols):
        pl.semaphore_signal(barrier, inc=1, device_id=(r, (c + k) % ncols), device_id_type=MESH)

    ang = angles[:, pl.ds(pl.multiple_of(r * n_obs, n_obs), n_obs)] * (1.0 / two_pi)
    sin_t, cos_t = sin_cos(ang[0:1])
    sin_p, cos_p = sin_cos(ang[1:2])
    e = jnp.concatenate([sin_t * cos_p, sin_t * sin_p, cos_t, jnp.zeros((5, n_obs), F32)], axis=0)
    left_a[pl.ds(n_rows, n_obs), :] = left_stack(e).T.astype(BF)
    cgeo[chip] = geometry[...]
    rgeo[c] = geometry[...]
    x2[chip // 2, chip % 2] = krylov[...]

    x = krylov[...]
    index = corr_index[...] - (r * ncols + c) * BLOCK
    base[...] = -0.5 * x.astype(F32) - correction(x, index, corr_weight[...])
    own = jnp.concatenate([geometry[...], jnp.zeros((1, BLOCK), F32)], axis=0)
    base[...] += incident(own, blades[...], harmonic[...])

    pl.semaphore_wait(barrier, nrows + ncols - 2)
    for k in range(1, nrows):
        peer = (r + k) % nrows
        at = (r + peer) % 2 * chips + chip
        send(geometry, cgeo.at[at], cgeo_sem.at[at], peer, c)
    for k in range(1, ncols):
        send(geometry, rgeo.at[c], rgeo_sem.at[c], r, (c + k) % ncols)

    for k in range(1, nrows):
        at = (chip + k) % nrows
        arrived(cgeo.at[at], cgeo_sem.at[at])
    for k in range(1, ncols):
        at = (c + k) % ncols
        arrived(rgeo.at[at], rgeo_sem.at[at])
    send(krylov, x2.at[(chips + chip) // 2, chip % 2], x_sem.at[chips + chip], sibling, c)
    for k in range(1, chips):
        peer = (chip + k) % chips * 2 + core
        send(krylov, x2.at[chip // 2, chip % 2], x_sem.at[chip], peer, c)
    g = jnp.concatenate([cgeo[i] for i in range(nrows)], axis=1)
    g = jnp.concatenate([g, jnp.zeros((1, n_cols), F32)], axis=0)
    for ref, v in zip(rights, right_features(g)):
        ref[...] = v
    g = jnp.concatenate([rgeo[i] for i in range(ncols)], axis=1)
    g = jnp.concatenate([g, jnp.zeros((1, n_rows), F32)], axis=0)
    la, lb = left_features(g, 4.0 / panels)
    left_a[pl.ds(0, n_rows), :] = la.T.astype(BF)
    left_b[...] = lb.T.astype(BF)

    def make_geometry(panel, step, into):
        first, far, count = panel
        cols = pl.ds(pl.multiple_of(step * COLS, COLS), COLS)
        rows = pl.ds(pl.multiple_of(first, BLOCK), count)
        top = pl.ds(0, count)
        la = left_a[rows, :]
        if far:
            into[0][top, :] = dot(la, rights[3][:, cols])
            into[1][top, :] = dot(la, rights[4][:, cols])
        else:
            into[0][top, :] = dot(la, rights[0][:, cols])
            into[1][top, :] = dot(la, rights[1][:, cols])
            into[2][top, :] = dot(left_b[rows, :], rights[2][:, cols])

    def make_values(panel, step, frm, tile):
        _, far, count = panel
        top = pl.ds(0, count)
        if far:
            re, im = far_values(frm[0][top, :], frm[1][top, :])
        else:
            re, im = operator_tile(frm[0][top, :], frm[1][top, :], frm[2][top, :])
        for h in range(half):
            tile[step * 2 * half + h, top, :] = re[:, h * LANES : (h + 1) * LANES]
            tile[step * 2 * half + half + h, top, :] = im[:, h * LANES : (h + 1) * LANES]

    def product(step, tile, rows):
        lhs = jnp.concatenate([tile[step * 2 * half + h, rows, :] for h in range(2 * half)], axis=1)
        return dot(lhs, x2[step].reshape(2 * COLS, x2.shape[-1]))

    every = pl.ds(0, ROWS)
    pair = c // 2
    far_z, near_z = (1 - pair // 2) * 2, pair // 2 * 2
    where = [far_z + pair % 2, far_z + 1 - pair % 2, near_z + 1 - pair % 2, pair]
    partner = c + 1 - 2 * (c % 2)
    seq = [(n_rows, True, ROWS)] + [(w * ROWS, False, ROWS) for w in where[:-1]]
    seq += [(partner * BLOCK, False, BLOCK), (c * BLOCK, False, BLOCK)]

    def prepare(step):
        for b in range(2):
            x2[step, 2 + b] = turned(x2[step, b])

    def two_steps(ph, h, products, between=None):
        for par in range(2):
            step = 2 * h + par
            make_geometry(seq[ph], lax.rem(step + 1, steps), planes[1 - par])
            if par == 0 and between is not None:
                between()
            make_values(seq[ph], step, planes[par], tiles[ph % 4])
            for which, at, total, rows in products(step, par):
                total[rows, :] += product(at, tiles[which % 4], rows)

    def run(ph, products, first_h=0, last_h=steps // 2):
        @pl.loop(first_h, last_h)
        def _(h):
            two_steps(ph, h, products)

    def pass_on():
        for k in range(1, chips):
            at = (chip + chips - k) % chips
            arrived(x2.at[at // 2, at % 2], x_sem.at[at])
            forward(k, at).start()
        for step in range(steps // 2):
            prepare(step)

    def take_passed():
        for k in range(chips, nrows):
            arrived(x2.at[k // 2, k % 2], x_sem.at[k])
        for step in range(steps // 2, steps):
            prepare(step)

    def send_parts(block):
        for b in range(2):
            owner = where[block] * 2 + b
            send(stage.at[owner], part_in.at[c], part_sem.at[c], r, owner)

    def keep_parts(block, total):
        for b in range(2):
            stage[where[block] * 2 + b] = total[pl.ds(b * BLOCK, BLOCK), :].astype(BF)

    def send_far():
        for k in range(1, ncols):
            owner = (c + k) % ncols
            rows = pl.ds(pl.multiple_of(owner * obs, obs), obs)
            send(far_stage.at[rows, :], far_in.at[c], far_sem.at[c], r, owner)

    top = pl.ds(0, BLOCK)
    for ph in range(len(seq)):
        make_geometry(seq[ph], 0, planes[0])
        if ph < 2:
            run(ph, lambda step, par: ())
        elif ph == 2:
            run(ph, lambda step, par: (), 0, steps // 4)
            pass_on()
            accs[0][...] = jnp.zeros_like(accs[0])
            run(ph, lambda step, par: ((0, step - steps // 2, accs[0], every),), steps // 4, steps // 2)
        elif ph == 3:
            take_passed()
            for total in accs[1:]:
                total[...] = jnp.zeros_like(total)
            listed = [(0, at, accs[0], every) for at in range(steps // 2, steps)]
            listed += [(w, at, accs[w], every) for w in (1, 2) for at in range(steps)]
            each = len(listed) // (steps // 2)
            more = (each + 1) // 2
            for h in range(steps // 2):
                todo = listed[h * each : (h + 1) * each]
                between = None
                if h == 1:
                    far_stage[...] = accs[0][...]
                    between = send_far
                if h == 3:
                    keep_parts(0, accs[1])
                    between = functools.partial(send_parts, 0)
                two_steps(ph, h, lambda step, par, todo=todo: todo[more:] if par else todo[:more], between)
            keep_parts(1, accs[2])
        elif ph == 4:
            accs[0][...] = jnp.zeros_like(accs[0])
            send_parts(1)
            run(ph, lambda step, par: ((3, step, accs[0], every),))
            keep_parts(2, accs[0])
        else:
            accs[1][top, :] = jnp.zeros((BLOCK, acc.shape[1]), F32)
            send_parts(2)
            run(ph, lambda step, par: ((4, step, accs[1], top),))
            stage[partner] = accs[1][top, :].astype(BF)

    tile = tiles[(len(seq) - 1) % 4]
    same = lax.broadcasted_iota(jnp.int32, (BLOCK, LANES), 0)
    lane = lax.broadcasted_iota(jnp.int32, (BLOCK, LANES), 1)
    for h in range(BLOCK // LANES):
        for part in range(2):
            at = chip // 2 * 2 * half + part * half + chip % 2 * (BLOCK // LANES) + h
            v = tile[at, top, :].astype(F32)
            tile[at, top, :] = jnp.where(same == lane + h * LANES, 0.0, v).astype(BF)

    mine = acc.at[top, :]
    mine[...] = product(0, tile, top)
    send(stage.at[partner], part_in.at[c], part_sem.at[c], r, partner)

    @pl.loop(1, steps)
    def _(step):
        mine[...] += product(step, tile, top)

    total = far_stage[pl.ds(pl.multiple_of(c * obs, obs), obs), :]
    for k in range(1, ncols):
        at = (c + ncols - k) % ncols
        arrived(far_in.at[at], far_sem.at[at])
        total += far_in[at]
    far_out[...] = total
    total = base[...] - mine[...]
    for k in range(1, ncols):
        at = (c + ncols - k) % ncols
        arrived(part_in.at[at], part_sem.at[at])
        total -= part_in[at].astype(F32)
    out[...] = total
    for copy in sends:
        copy.wait_send()
    for k in range(1, chips):
        forward(k, (chip + chips - k) % chips).wait_send()


def local(krylov, geometry, corr_index, corr_weight, blades, harmonic, observer_angles):
    nrows = lax.axis_size("rows")
    ncols = lax.axis_size("cols")
    width = krylov.shape[1]
    n_cols, n_rows = nrows * BLOCK, ncols * BLOCK
    n_obs = observer_angles.shape[1] // nrows
    n_sends = (nrows - 1) + 4 * (ncols - 1) + nrows
    scoped = (
        [pltpu.VMEM((n_rows + n_obs, 48), BF), pltpu.VMEM((n_rows, 48), BF)]
        + [pltpu.VMEM((48, n_cols), BF)] * 5
        + [pltpu.VMEM((2 * n_cols // LANES, ROWS, LANES), BF)] * 4
    )

    def body(*refs):
        pl.run_scoped(lambda *own: kernel(nrows, ncols, *own, *refs), *scoped)

    vm = pl.BlockSpec(memory_space=pltpu.VMEM)
    dma = pltpu.SemaphoreType.DMA
    return pl.pallas_call(
        body,
        out_shape=(
            jax.ShapeDtypeStruct((BLOCK, width), F32),
            jax.ShapeDtypeStruct((n_obs // ncols, width), F32),
        ),
        in_specs=[vm] * 7,
        out_specs=(vm, vm),
        scratch_shapes=[
            pltpu.VMEM((nrows, 7, BLOCK), F32),
            pltpu.VMEM((ncols, 7, BLOCK), F32),
        ]
        + [pltpu.VMEM((n_cols // COLS, 4, BLOCK, width), BF)]
        + [pltpu.VMEM((ROWS, COLS), F32)] * 6
        + [
            pltpu.VMEM((ROWS, width), F32),
            pltpu.VMEM((ROWS, width), F32),
            pltpu.VMEM((ROWS, width), F32),
            pltpu.VMEM((BLOCK, width), F32),
            pltpu.VMEM((ncols, BLOCK, width), BF),
            pltpu.VMEM((n_obs, width), F32),
            pltpu.VMEM((ncols, BLOCK, width), BF),
            pltpu.VMEM((ncols, n_obs // ncols, width), F32),
            dma((n_sends,)),
            dma((nrows,)),
            dma((ncols,)),
            dma((nrows,)),
            dma((ncols,)),
            dma((ncols,)),
        ],
        compiler_params=pltpu.CompilerParams(
            collective_id=0, has_side_effects=True, vmem_limit_bytes=60 << 20
        ),
        name="burton_miller",
    )(krylov, geometry, corr_index, corr_weight, blades[None], harmonic[None], observer_angles)


def solution(mesh):
    placed = (
        P(("rows", "cols"), None),
        P(None, ("rows", "cols")),
        P(None, ("rows", "cols")),
        P(None, ("rows", "cols")),
        P(),
        P(),
        P(),
    )
    return jax.shard_map(
        local,
        mesh=mesh,
        in_specs=placed,
        out_specs=(P(("rows", "cols"), None), P(("rows", "cols"), None)),
        check_vma=False,
    )
```
